256 devices in a mesh: obs: 8 (over z_hi, core), gx: 8 (over y, z_lo), gy: 4 (over x).
Axes of the slice: x: 4, y: 4, z: 8 (z_hi: 4, z_lo: 2; z = z_hi * 2 + z_lo), core: 2. Of those that a mesh axis runs over, the one named last changes fastest.
Arguments:
- closing_costates: float32 [2, 32, 64, 64, 128], P(None, 'obs', 'gx', 'gy'), may hold values from -6.5 to 6.5
- saved_pore_load: float32 [3, 64, 64, 128], P(None, 'gx', 'gy', 'obs'), may hold values from -4 to 4
- saved_heat_field: float32 [3, 64, 64, 128], P(None, 'gx', 'gy', 'obs'), may hold values from -2.5 to -0.5
- saved_dilatation: float32 [3, 64, 64, 128], P(None, 'gx', 'gy', 'obs'), may hold values from -2.5 to -0.5
- saved_conductivity: float32 [3, 64, 64, 128], P(None, 'gx', 'gy', 'obs'), may hold values from 2.5 to 5
- data_residual: float32 [3, 32, 128], P(None, 'obs'), may hold values from -8 to 8
- borehole_flat_position: int32 [32], P('obs'), may hold values from 0 to 4095
- probe_multiplier: int32 [32], P('obs'), may hold values from 1 to 4
Outputs:
- adjoint_start: float32 [2, 32, 64, 64, 128], P(None, 'obs', 'gx', 'gy')
- gradient: float32 [64, 64, 128], P('gx', 'gy', 'obs')
The draws below stay inside these ranges and needn't reach their ends.
All inputs are finite; a program needn't handle non-finite values.
Results may differ from the reference program's by a relative error of at most 0.0003.
Values sent between devices are 32-bit elements; how exact they have to be, the bound alone decides.
A program may use at most 64 MiB of HBM per device.

```python
import math
import jax
import jax.numpy as jnp
from jax import lax

GRID_LEN_THREE = 128
BACKWARD_COUNT = 3
ITERS = 4
GRID_LEN_ONE = 64
GRID_LEN_TWO = 64
OBSERVATIONS = 32


def draw_closing_costates(key, part):
    key_amp = jax.random.fold_in(key, 11)
    key_sign = jax.random.fold_in(key, 12)
    key_noise = jax.random.fold_in(key, 13)
    full_shape = (2, OBSERVATIONS, GRID_LEN_ONE, GRID_LEN_TWO, GRID_LEN_THREE)
    level_shape = (2, OBSERVATIONS, 1, 1, 1)
    signs = (2 * jax.random.randint(key_sign, level_shape, 0, 2) - 1).astype(jnp.float32)
    amplitude = jax.random.uniform(key_amp, level_shape, jnp.float32, 4.0, 5.5)
    smooth = signs * amplitude
    noise = 0.5 * jnp.clip(jax.random.normal(key_noise, full_shape, jnp.float32), -2.0, 2.0)
    return (smooth + noise).astype(jnp.float32)


def with_ends(result, own_key, smallest, high):
    shape = result.shape
    place = [jax.random.randint(jax.random.fold_in(own_key, axis), (), 0, shape[axis]) for axis in range(len(shape))]
    result = result.at[tuple(place)].set(smallest)
    longest = shape.index(max(shape))
    place[longest] = (place[longest] + 1) % shape[longest]
    return result.at[tuple(place)].set(high)


def steps_of(rng, extent, shards, smallest, top_value):
    level = 1.0
    for axis_at, blocks in shards:
        heights = jax.random.uniform(jax.random.fold_in(jax.random.fold_in(rng, 6), axis_at), (blocks,), jnp.float32, smallest / len(shards), top_value / len(shards))
        level = level * jnp.repeat(jnp.exp(heights), extent[axis_at] // blocks).reshape((-1,) + (1,) * (len(extent) - 1 - axis_at))
    return level


def centred(key, dims, scale, bound, cuts=(), kind=jnp.bfloat16):
    level = steps_of(key, dims, cuts, -0.22, 0.18) if cuts else 1.0
    values = jax.random.normal(key, dims, jnp.float32) * scale * level
    return jnp.minimum(jnp.maximum(values, -bound), bound).astype(kind)


def setup_inputs(seed: int = 0) -> dict:
    arg_keys = jax.random.split(jax.random.key(seed), 9)
    return {
        "closing_costates": draw_closing_costates(jax.random.fold_in(arg_keys[8], 71), 0),
        "saved_pore_load": centred(arg_keys[1], (BACKWARD_COUNT, GRID_LEN_ONE, GRID_LEN_TWO, GRID_LEN_THREE), 1.0, 4.0, ((1, 8), (2, 4), (3, 8)), jnp.float32),
        "saved_heat_field": jnp.clip(-2.5 + 2.0 * jax.random.uniform(arg_keys[2], (BACKWARD_COUNT, GRID_LEN_ONE, GRID_LEN_TWO, GRID_LEN_THREE), jnp.float32) ** steps_of(arg_keys[2], (BACKWARD_COUNT, GRID_LEN_ONE, GRID_LEN_TWO, GRID_LEN_THREE), ((1, 8), (2, 4), (3, 8)), -0.2, 0.2), -2.5, -0.5),
        "saved_dilatation": jnp.clip(-2.5 + 2.0 * jax.random.uniform(arg_keys[3], (BACKWARD_COUNT, GRID_LEN_ONE, GRID_LEN_TWO, GRID_LEN_THREE), jnp.float32) ** steps_of(arg_keys[3], (BACKWARD_COUNT, GRID_LEN_ONE, GRID_LEN_TWO, GRID_LEN_THREE), ((1, 8), (2, 4), (3, 8)), -0.2, 0.2), -2.5, -0.5),
        "saved_conductivity": jnp.clip(jnp.exp(math.log(5.0) - 0.6931472 * jax.random.uniform(arg_keys[4], (BACKWARD_COUNT, GRID_LEN_ONE, GRID_LEN_TWO, GRID_LEN_THREE), jnp.float32) ** steps_of(arg_keys[4], (BACKWARD_COUNT, GRID_LEN_ONE, GRID_LEN_TWO, GRID_LEN_THREE), ((1, 8), (2, 4), (3, 8)), -0.2, 0.2)), 2.5, 5.0),
        "data_residual": centred(arg_keys[5], (BACKWARD_COUNT, OBSERVATIONS, GRID_LEN_THREE), 2.0, 8.0, ((1, 8),), jnp.float32),
        "borehole_flat_position": with_ends(jax.random.randint(arg_keys[6], (OBSERVATIONS,), 0, GRID_LEN_ONE * GRID_LEN_TWO), jax.random.fold_in(arg_keys[6], 1), 0, (GRID_LEN_ONE * GRID_LEN_TWO) - 1).astype(jnp.int32),
        "probe_multiplier": with_ends(jax.random.randint(arg_keys[7], (OBSERVATIONS,), 1, 5), jax.random.fold_in(arg_keys[7], 1), 1, 4).astype(jnp.int32),
    }


heat_diffusivity = 2.0


def neighbour_sum(field):
    padded = jnp.pad(field, ((1, 1), (1, 1), (1, 1)))
    summed = padded[2:, 1:-1, 1:-1] + padded[:-2, 1:-1, 1:-1]
    summed = summed + padded[1:-1, 2:, 1:-1] + padded[1:-1, :-2, 1:-1]
    return summed + padded[1:-1, 1:-1, 2:] + padded[1:-1, 1:-1, :-2]


def reference(closing_costates, saved_pore_load, saved_heat_field, saved_dilatation, saved_conductivity, data_residual, borehole_flat_position, probe_multiplier):
    flat_index = jnp.arange(GRID_LEN_ONE, dtype=jnp.int32)[:, None] * GRID_LEN_TWO + jnp.arange(GRID_LEN_TWO, dtype=jnp.int32)[None, :]

    def one_observation(gradient, scanned):
        adj_p, heat_costate, misfit_obs, well, weight = scanned
        well_mask = (flat_index == well).astype(jnp.float32)[:, :, None]
        for backward_counter in range(BACKWARD_COUNT - 1, -1, -1):
            perm_now = saved_conductivity[backward_counter]
            pressure_now = saved_pore_load[backward_counter]
            store_p = jnp.exp(saved_dilatation[backward_counter])
            kept_heat_field = jnp.exp(0.5 * saved_heat_field[backward_counter])
            coupling = 0.2 * jnp.tanh(pressure_now)
            diag_p = store_p + 6.0 * perm_now
            heat_main_entry = kept_heat_field + 6.0 * heat_diffusivity
            right_p = store_p * adj_p + well_mask * misfit_obs[backward_counter][None, None, :]
            heat_source_term = kept_heat_field * heat_costate
            for sweep_index in range(ITERS):
                near_p = neighbour_sum(adj_p)
                near_t = neighbour_sum(heat_costate)
                adj_p = (right_p + perm_now * near_p + coupling * heat_costate) / diag_p
                heat_costate = (heat_source_term + heat_diffusivity * near_t + coupling * adj_p) / heat_main_entry
            laplace = neighbour_sum(pressure_now) - 6.0 * pressure_now
            gradient = gradient + weight * perm_now * laplace * adj_p
        return gradient, (adj_p, heat_costate)

    scanned = (closing_costates[0], closing_costates[1], jnp.transpose(data_residual, (1, 0, 2)), borehole_flat_position,
               probe_multiplier.astype(jnp.float32))
    start = jnp.zeros((GRID_LEN_ONE, GRID_LEN_TWO, GRID_LEN_THREE), jnp.float32)
    gradient, (all_p, all_t) = lax.scan(one_observation, start, scanned)
    return jnp.stack([all_p, all_t]), gradient
```

```python
import functools

import jax
import jax.numpy as jnp
from jax import lax
from jax.experimental import pallas as pl
from jax.experimental.pallas import tpu as pltpu
from jax.sharding import PartitionSpec as P

MESH = pl.DeviceIdType.MESH
F32 = jnp.float32
ITERS = 4
NX, NY, NZ = 8, 16, 128
NS = 3
NO = 4
NP = 8
LP = NZ // NP
NJ = 8
AP, BP, AT, BT = range(4)
RPC, IP, RTC, KK = range(4)


def role(obs, gx):
    return 2 * (obs // 2) + gx % 2, 2 * (gx // 2) + obs % 2


def regroup(tiles, lane_group):
    turned = [pltpu.roll(t, LP * d, 1) if d else t for d, t in enumerate(tiles)]
    outs = []
    for x in range(NP):
        mixed = turned[(NP - 1 - x) % NP]
        for g in range(NP - 1):
            mixed = jnp.where(lane_group == g, turned[(g - x) % NP], mixed)
        outs.append(pltpu.roll(mixed, NZ - LP * x, 1) if x else mixed)
    return outs


def kernel(
    cost_ref, pore_ref, heat_ref, dil_ref, cond_ref, resid_ref, pos_ref, wgt_ref,
    out_ref, grad_ref,
    saved, pack, gath, raw, meta, meta_in, state, ysend, yrecv, coef, crep, prep_pore, ypore, ycol, prow, pcol,
    right, gacc, gpack, gred, outst,
    load_sem, gsend, grecv, ssend, srecv, msem, hsend, hrecv, psend, precv, osend, orecv, rsend, rrecv,
):
    obs, gx, gy = lax.axis_index("obs"), lax.axis_index("gx"), lax.axis_index("gy")
    lobs, lgx = role(obs, gx)
    stays = jnp.logical_and(lobs == obs, lgx == gx)
    moves = jnp.logical_not(stays)
    zh, yy = obs // 2, gx // 2
    ngx, ngy = lax.axis_size("gx"), lax.axis_size("gy")

    lane = lax.broadcasted_iota(jnp.int32, (8, NZ), 1)
    sub = lax.broadcasted_iota(jnp.int32, (8, NZ), 0)
    lane_group = lane // LP
    first_lane, last_lane = lane == 0, lane == NZ - 1
    even = sub % 2 == 0

    exists = (lgx > 0, lgx < ngx - 1, gy > 0, gy < ngy - 1)
    xm = role(lobs, jnp.maximum(lgx - 1, 0))
    xp = role(lobs, jnp.minimum(lgx + 1, ngx - 1))
    near = (
        (xm[0], xm[1], gy),
        (xp[0], xp[1], gy),
        (obs, gx, jnp.maximum(gy - 1, 0)),
        (obs, gx, jnp.minimum(gy + 1, ngy - 1)),
    )
    partner = (lobs, lgx, gy)

    fields = (pore_ref, heat_ref, dil_ref, cond_ref)

    def load(n, f):
        return pltpu.make_async_copy(fields[f].at[n], saved.at[n, f], load_sem.at[n, f])

    for n in range(NS - 1, -1, -1):
        for f in range(4):
            load(n, f).start()

    zero = jnp.zeros((8, NZ), F32)
    for slot in range(2):
        for row in (0, NX + 1):
            state[slot, row] = jnp.zeros((2 * NJ * 8, NZ), F32)
    yrecv[...] = jnp.zeros(yrecv.shape, F32)
    prow[...] = jnp.zeros(prow.shape, F32)
    pcol[...] = jnp.zeros(pcol.shape, F32)

    barrier = pltpu.get_barrier_semaphore()
    for zz in range(4):
        for core in range(2):
            for low in range(2):
                there = (2 * zz + core, 2 * yy + low, gy)

                @pl.when(jnp.logical_or(there[0] != obs, there[1] != gx))
                def _(there=there):
                    pl.semaphore_signal(barrier, inc=1, device_id=there, device_id_type=MESH)

    for k in range(4):

        @pl.when(exists[k])
        def _(k=k):
            pl.semaphore_signal(barrier, inc=1, device_id=near[k], device_id_type=MESH)

    count = 15
    for k in range(4):
        count = count + exists[k].astype(jnp.int32)
    pl.semaphore_wait(barrier, count)

    srow = sub // 2
    for n in range(NS):
        tile = zero
        for o in range(NO):
            tile = jnp.where(srow == o, jnp.broadcast_to(resid_ref[n, o : o + 1, :], (8, NZ)), tile)
        meta[n] = tile
    pos = jnp.zeros((8, NZ), jnp.int32)
    wgt = jnp.zeros((8, NZ), jnp.int32)
    for o in range(NO):
        pos = jnp.where(srow == o, pos_ref[o], pos)
        wgt = jnp.where(srow == o, wgt_ref[o], wgt)
    meta[3] = pos.astype(F32)
    meta[4] = wgt.astype(F32)

    def gather_copy(n, target):
        return pltpu.make_async_remote_copy(
            src_ref=pack.at[n],
            dst_ref=gath.at[n, obs],
            send_sem=gsend.at[n, target],
            recv_sem=grecv.at[n, obs],
            device_id=(2 * (target // 2) + gx % 2, 2 * yy + target % 2, gy),
            device_id_type=MESH,
        )

    def is_me(target):
        return jnp.logical_and(stays, lobs == target)

    def send_saved(n):
        for f in range(4):
            load(n, f).wait()
        for f in range(4):
            for h in range(2):
                packed = saved_tile(n, f, 0, h)
                for x in range(1, NX):
                    packed = jnp.where(
                        lane_group == x, pltpu.roll(saved_tile(n, f, x, h), LP * x, 1), packed
                    )
                pack[n, pl.ds((f * 2 + h) * 8, 8), :] = packed

                @pl.when(stays)
                def _(packed=packed, f=f, h=h):
                    gath[n, obs, pl.ds((f * 2 + h) * 8, 8), :] = packed

        for target in range(NP):

            @pl.when(jnp.logical_not(is_me(target)))
            def _(target=target):
                gather_copy(n, target).start()

    def saved_tile(n, f, x, h):
        piece = saved[n, f, x, pl.ds(h * 8, 8), :]
        return jnp.concatenate([piece, jnp.zeros((8, NZ - LP), F32)], axis=1)

    def swap_in(k):
        return pltpu.make_async_remote_copy(
            src_ref=cost_ref.at[k // NO, k % NO],
            dst_ref=raw.at[:, pl.ds(k * NY, NY), :],
            send_sem=ssend.at[k],
            recv_sem=srecv.at[k],
            device_id=partner,
            device_id_type=MESH,
        )

    def keep_in(k):
        return pltpu.make_async_copy(
            cost_ref.at[k // NO, k % NO], raw.at[:, pl.ds(k * NY, NY), :], srecv.at[k]
        )

    def send_meta():
        return pltpu.make_async_remote_copy(
            src_ref=meta, dst_ref=meta_in, send_sem=msem.at[0], recv_sem=msem.at[1], device_id=partner, device_id_type=MESH
        )

    send_saved(NS - 1)

    @pl.when(moves)
    def _():
        send_meta().start()
        for k in range(2 * NO):
            swap_in(k).start()

    @pl.when(stays)
    def _():
        for k in range(2 * NO):
            keep_in(k).start()
        meta_in[...] = meta[...]

    for n in range(NS - 2, -1, -1):
        send_saved(n)

    @pl.when(moves)
    def _():
        send_meta().wait()
        for k in range(2 * NO):
            swap_in(k).wait()

    @pl.when(stays)
    def _():
        for k in range(2 * NO):
            keep_in(k).wait()

    def halo(slot, k):
        if k == 0:
            src, dst = state.at[slot, 1], state.at[slot, NX + 1]
        elif k == 1:
            src, dst = state.at[slot, NX], state.at[slot, 0]
        elif k == 2:
            src, dst = ysend.at[slot, 0], yrecv.at[slot, 1]
        else:
            src, dst = ysend.at[slot, 1], yrecv.at[slot, 0]
        return pltpu.make_async_remote_copy(
            src_ref=src,
            dst_ref=dst,
            send_sem=hsend.at[slot, k],
            recv_sem=hrecv.at[slot, k ^ 1],
            device_id=near[k],
            device_id_type=MESH,
        )

    def start_halos(slot):
        for k in range(4):

            @pl.when(exists[k])
            def _(k=k):
                halo(slot, k).start()

    def wait_halos(slot):
        for k in range(4):

            @pl.when(exists[k])
            def _(k=k):
                halo(slot, k ^ 1).wait_recv()
                halo(slot, k).wait_send()

    def y_message(slot, x, p, t):
        ysend[slot, 0, pl.ds(x * 8, 8), :] = jnp.where(even, p[0], pltpu.roll(t[0], 1, 0))
        ysend[slot, 1, pl.ds(x * 8, 8), :] = jnp.where(even, pltpu.roll(p[1], 7, 0), t[1])

    def first_row(x, _):
        ends = []
        for f in range(2):
            tiles = [raw[x, pl.ds(f * 64 + j, 8, stride=8), :] for j in range(NJ)]
            for j in range(NJ):
                state[0, x + 1, pl.ds((f * NJ + j) * 8, 8), :] = tiles[j]
            ends.append((tiles[0], tiles[-1]))
        y_message(0, x, *ends)
        return 0

    lax.fori_loop(0, NX, first_row, 0)
    start_halos(0)

    def around(tiles, up, down, before, after):
        sums = []
        for j in range(NJ):
            here = tiles[j]
            total = up[j] + down[j]
            total = total + (tiles[j - 1] if j else before) + (tiles[j + 1] if j < NJ - 1 else after)
            deep = jnp.where(first_lane, 0.0, pltpu.roll(here, 1, 1))
            shallow = jnp.where(last_lane, 0.0, pltpu.roll(here, NZ - 1, 1))
            sums.append(total + deep + shallow)
        return sums

    def relax_row(slot, x, last):
        tiles = [[state[slot, x + 1, pl.ds((f * NJ + j) * 8, 8), :] for j in range(NJ)] for f in range(2)]
        up = [[state[slot, x, pl.ds((f * NJ + j) * 8, 8), :] for j in range(NJ)] for f in range(2)]
        down = [[state[slot, x + 2, pl.ds((f * NJ + j) * 8, 8), :] for j in range(NJ)] for f in range(2)]
        low = yrecv[slot, 0, pl.ds(x * 8, 8), :]
        high = yrecv[slot, 1, pl.ds(x * 8, 8), :]
        lows = (low, pltpu.roll(low, 7, 0))
        highs = (pltpu.roll(high, 1, 0), high)
        sums = []
        for f in range(2):
            before = jnp.where(even, lows[f], pltpu.roll(tiles[f][-1], 1, 0))
            after = jnp.where(even, pltpu.roll(tiles[f][0], 7, 0), highs[f])
            sums.append(around(tiles[f], up[f], down[f], before, after))
        ends = [[], []]
        for j in range(NJ):
            at = pl.ds(j * 8, 8)
            new_p = (
                right[x, at, :] + coef[AP, x, at, :] * sums[0][j] + coef[BP, x, at, :] * tiles[1][j]
            )
            new_t = (
                right[x, pl.ds((NJ + j) * 8, 8), :]
                + coef[AT, x, at, :] * sums[1][j]
                + coef[BT, x, at, :] * new_p
            )
            state[1 - slot, x + 1, at, :] = new_p
            state[1 - slot, x + 1, pl.ds((NJ + j) * 8, 8), :] = new_t
            if j in (0, NJ - 1):
                ends[0].append(new_p)
                ends[1].append(new_t)
        y_message(1 - slot, x, *ends)

    base_cell = (lgx * NX) * (ngy * NY) + gy * NY

    def pore_halo(n, k):
        if k == 0:
            src, dst = ypore.at[n, pl.ds(0, NY)], prow.at[n, 1]
        elif k == 1:
            src, dst = ypore.at[n, pl.ds((NX - 1) * NY, NY)], prow.at[n, 0]
        elif k == 2:
            src, dst = ycol.at[n, 0], pcol.at[n, 1]
        else:
            src, dst = ycol.at[n, 1], pcol.at[n, 0]
        return pltpu.make_async_remote_copy(
            src_ref=src,
            dst_ref=dst,
            send_sem=psend.at[n, k],
            recv_sem=precv.at[n, k ^ 1],
            device_id=near[k],
            device_id_type=MESH,
        )

    def repeat(ref, lead, h, value):
        for o in range(NO):
            ref[(*lead, pl.ds(o * NY + h * 8, 8), slice(None))] = value

    def prepare(n):
        for d in range(NP):

            @pl.when(jnp.logical_not(jnp.logical_and(stays, obs == d)))
            def _(d=d):
                pltpu.make_async_remote_copy(
                    src_ref=pack.at[n],
                    dst_ref=gath.at[n, d],
                    send_sem=gsend.at[n, d],
                    recv_sem=grecv.at[n, d],
                    device_id=partner,
                    device_id_type=MESH,
                ).wait_recv()

        for h in range(2):
            whole = [
                regroup([gath[n, d, pl.ds((f * 2 + h) * 8, 8), :] for d in range(NP)], lane_group) for f in range(4)
            ]
            for x in range(NX):
                pore, heat, dil, perm = (whole[f][x] for f in range(4))
                store_p = jnp.exp(dil)
                store_t = jnp.exp(0.5 * heat)
                coupling = 0.2 * jnp.tanh(pore)
                inv_p = 1.0 / (store_p + 6.0 * perm)
                inv_t = 1.0 / (store_t + 12.0)
                rows = {
                    0: perm * inv_p,
                    1: coupling * inv_p,
                    2: 2.0 * inv_t,
                    3: coupling * inv_t,
                    4: store_p * inv_p,
                    5: inv_p,
                    6: store_t * inv_t,
                    7: perm,
                }
                for c, value in rows.items():
                    repeat(crep, (c, x), h, value)
                repeat(prep_pore, (x + 1,), h, pore)
                ypore[n, pl.ds(x * NY + h * 8, 8), :] = pore
        for side, y in ((0, 0), (1, NY - 1)):
            ycol[n, side] = ypore[n, pl.ds(y, NX, stride=NY), :]
        for k in range(4):

            @pl.when(exists[k])
            def _(k=k):
                pore_halo(n, k).start()

        source = meta_in[n]
        cell = meta_in[3] - (8 * (sub % 2) + base_cell).astype(F32)

        def spread(x, _):
            for j in range(NJ):
                at = pl.ds(j * 8, 8)
                for c in range(4):
                    coef[c, x, at, :] = crep[c, x, pl.ds(j, 8, stride=8), :]
                mine = cell == (x * (ngy * NY) + j).astype(F32)
                term = jnp.where(mine, source, 0.0)
                right[x, at, :] = (
                    crep[4, x, pl.ds(j, 8, stride=8), :] * state[0, x + 1, at, :]
                    + crep[5, x, pl.ds(j, 8, stride=8), :] * term
                )
                right[x, pl.ds((NJ + j) * 8, 8), :] = (
                    crep[6, x, pl.ds(j, 8, stride=8), :] * state[0, x + 1, pl.ds((NJ + j) * 8, 8), :]
                )
            return 0

        lax.fori_loop(0, NX, spread, 0)

    def add_gradient(n):
        for k in range(4):

            @pl.when(exists[k])
            def _(k=k):
                pore_halo(n, k ^ 1).wait_recv()
                pore_halo(n, k).wait_send()

        for side, row in ((0, 0), (1, NX + 1)):
            for h in range(2):
                repeat(prep_pore, (row,), h, prow[n, side, pl.ds(h * 8, 8), :])
        weight = meta_in[4]

        def row(x, _):
            tiles, up, down = (
                [prep_pore[x + dx, pl.ds(j, 8, stride=8), :] for j in range(NJ)] for dx in (1, 0, 2)
            )
            low = jnp.broadcast_to(pcol[n, 0, pl.ds(x, 1), :], (8, NZ))
            high = jnp.broadcast_to(pcol[n, 1, pl.ds(x, 1), :], (8, NZ))
            before = jnp.where(even, low, pltpu.roll(tiles[-1], 1, 0))
            after = jnp.where(even, pltpu.roll(tiles[0], 7, 0), high)
            sums = around(tiles, up, down, before, after)
            for j in range(NJ):
                at = pl.ds(j * 8, 8)
                laplace = sums[j] - 6.0 * tiles[j]
                gacc[x, at, :] += (
                    crep[7, x, pl.ds(j, 8, stride=8), :] * laplace * (weight * state[0, x + 1, at, :])
                )
            return 0

        lax.fori_loop(0, NX, row, 0)

    def swap_out(k):
        return pltpu.make_async_remote_copy(
            src_ref=outst.at[:, pl.ds(k * NY, NY), :],
            dst_ref=out_ref.at[k // NO, k % NO],
            send_sem=osend.at[k],
            recv_sem=orecv.at[k],
            device_id=partner,
            device_id_type=MESH,
        )

    def keep_out(k):
        return pltpu.make_async_copy(
            outst.at[:, pl.ds(k * NY, NY), :], out_ref.at[k // NO, k % NO], orecv.at[k]
        )

    def finish():
        def row(x, _):
            for f in range(2):
                for o in range(NO):
                    for h in range(2):
                        outst[x, pl.ds((f * NO + o) * NY + h * 8, 8), :] = state[
                            0, x + 1, pl.ds(f * 64 + 2 * o + h, 8, stride=8), :
                        ]
            return 0

        lax.fori_loop(0, NX, row, 0)

        @pl.when(moves)
        def _():
            for k in range(2 * NO):
                swap_out(k).start()

        @pl.when(stays)
        def _():
            for k in range(2 * NO):
                keep_out(k).start()

    gacc[...] = jnp.zeros(gacc.shape, F32)

    def step(i, _):
        n = NS - 1 - i
        prepare(n)
        for sweep in range(ITERS):
            slot = sweep % 2
            wait_halos(slot)

            def row(x, _, slot=slot):
                relax_row(slot, x, False)
                return 0

            lax.fori_loop(0, NX, row, 0, unroll=2)
            if sweep < ITERS - 1:
                start_halos(1 - slot)

        @pl.when(n > 0)
        def _():
            start_halos(0)

        @pl.when(n == 0)
        def _():
            finish()

        add_gradient(n)
        return 0

    lax.fori_loop(0, NS, step, 0)

    for h in range(2):
        whole = []
        for x in range(NX):
            total = gacc[x, pl.ds(h, 8, stride=8), :]
            for o in range(1, NO):
                total = total + gacc[x, pl.ds(2 * o + h, 8, stride=8), :]
            whole.append(total)
        for d, tile in enumerate(regroup(whole, lane_group)):
            gpack[d, pl.ds(h * 8, 8), :] = tile

            @pl.when(jnp.logical_and(stays, obs == d))
            def _(tile=tile, h=h):
                gred[lobs, pl.ds(h * 8, 8), :] = tile

    def reduce_copy(d):
        return pltpu.make_async_remote_copy(
            src_ref=gpack.at[d],
            dst_ref=gred.at[lobs],
            send_sem=rsend.at[d],
            recv_sem=rrecv.at[lobs],
            device_id=(d, lgx, gy),
            device_id_type=MESH,
        )

    for d in range(NP):

        @pl.when(jnp.logical_not(jnp.logical_and(stays, obs == d)))
        def _(d=d):
            reduce_copy(d).start()

    for d in range(NP):

        @pl.when(jnp.logical_not(is_me(d)))
        def _(d=d):
            pltpu.make_async_remote_copy(
                src_ref=gpack.at[d],
                dst_ref=gred.at[d],
                send_sem=rsend.at[d],
                recv_sem=rrecv.at[d],
                device_id=partner,
                device_id_type=MESH,
            ).wait_recv()

    for h in range(2):
        total = gred[0, pl.ds(h * 8, 8), :]
        for d in range(1, NP):
            total = total + gred[d, pl.ds(h * 8, 8), :]
        for x in range(NX):
            turned = pltpu.roll(total, NZ - LP * x, 1) if x else total
            grad_ref[x, pl.ds(h * 8, 8), :] = turned[:, :LP]

    for d in range(NP):

        @pl.when(jnp.logical_not(jnp.logical_and(stays, obs == d)))
        def _(d=d):
            reduce_copy(d).wait_send()

    for n in range(NS):
        for target in range(NP):

            @pl.when(jnp.logical_not(is_me(target)))
            def _(n=n, target=target):
                gather_copy(n, target).wait_send()

    @pl.when(moves)
    def _():
        for k in range(2 * NO):
            swap_out(k).wait()

    @pl.when(stays)
    def _():
        for k in range(2 * NO):
            keep_out(k).wait()


def local(*args):
    hbm = pl.BlockSpec(memory_space=pl.ANY)
    vmem = pl.BlockSpec(memory_space=pltpu.VMEM)
    smem = pl.BlockSpec(memory_space=pltpu.SMEM)
    dma = pltpu.SemaphoreType.DMA
    rows = 2 * NJ * 8
    return pl.pallas_call(
        kernel,
        out_shape=(
            jax.ShapeDtypeStruct((2, NO, NX, NY, NZ), F32),
            jax.ShapeDtypeStruct((NX, NY, LP), F32),
        ),
        in_specs=[hbm, hbm, hbm, hbm, hbm, vmem, smem, smem],
        out_specs=(hbm, vmem),
        scratch_shapes=[
            pltpu.VMEM((NS, 4, NX, NY, LP), F32),
            pltpu.VMEM((NS, 64, NZ), F32),
            pltpu.VMEM((NS, NP, 64, NZ), F32),
            pltpu.VMEM((NX, rows, NZ), F32),
            pltpu.VMEM((5, 8, NZ), F32),
            pltpu.VMEM((5, 8, NZ), F32),
            pltpu.VMEM((2, NX + 2, rows, NZ), F32),
            pltpu.VMEM((2, 2, NX * 8, NZ), F32),
            pltpu.VMEM((2, 2, NX * 8, NZ), F32),
            pltpu.VMEM((4, NX, 64, NZ), F32),
            pltpu.VMEM((8, NX, 64, NZ), F32),
            pltpu.VMEM((NX + 2, 64, NZ), F32),
            pltpu.VMEM((NS, NX * NY, NZ), F32),
            pltpu.VMEM((NS, 2, 8, NZ), F32),
            pltpu.VMEM((NS, 2, NY, NZ), F32),
            pltpu.VMEM((NS, 2, 8, NZ), F32),
            pltpu.VMEM((NX, rows, NZ), F32),
            pltpu.VMEM((NX, 64, NZ), F32),
            pltpu.VMEM((NP, NY, NZ), F32),
            pltpu.VMEM((NP, NY, NZ), F32),
            pltpu.VMEM((NX, rows, NZ), F32),
            dma((NS, 4)),
            dma((NS, NP)),
            dma((NS, NP)),
            dma((2 * NO,)),
            dma((2 * NO,)),
            dma((2,)),
            dma((2, 4)),
            dma((2, 4)),
            dma((NS, 4)),
            dma((NS, 4)),
            dma((2 * NO,)),
            dma((2 * NO,)),
            dma((NP,)),
            dma((NP,)),
        ],
        compiler_params=pltpu.CompilerParams(
            collective_id=0, has_side_effects=True, vmem_limit_bytes=48 * 1024 * 1024
        ),
    )(*args)


def solution(mesh):
    return jax.shard_map(
        local,
        mesh=mesh,
        in_specs=(
            P(None, "obs", "gx", "gy", None),
            P(None, "gx", "gy", "obs"),
            P(None, "gx", "gy", "obs"),
            P(None, "gx", "gy", "obs"),
            P(None, "gx", "gy", "obs"),
            P(None, "obs", None),
            P("obs"),
            P("obs"),
        ),
        out_specs=(P(None, "obs", "gx", "gy", None), P("gx", "gy", "obs")),
        check_vma=False,
    )
```

```python
import functools

import jax
import jax.numpy as jnp
from jax import lax
from jax.experimental import pallas as pl
from jax.experimental.pallas import tpu as pltpu
from jax.sharding import PartitionSpec as P

MESH = pl.DeviceIdType.MESH
F32 = jnp.float32
ITERS = 4
UNROLL = 2
NX, NY, NZ = 8, 16, 128
NS = 3
NO = 4
NP = 8
LP = NZ // NP
SO = 2
ST = NO // SO
NQ = 8 // SO
NJ = NY // NQ
NG = NQ // 2
XG = NX // NG
ROWS = 2 * NJ * 8
AP, BP, AT, BT, RPC, IP, RTC, KK = range(8)


def role(obs, gx):
    return 2 * (obs // 2) + gx % 2, 2 * (gx // 2) + obs % 2


def regroup(tiles, lane_group):
    turned = [pltpu.roll(t, LP * d, 1) if d else t for d, t in enumerate(tiles)]
    outs = []
    for x in range(NP):
        mixed = turned[(NP - 1 - x) % NP]
        for g in range(NP - 1):
            mixed = jnp.where(lane_group == g, turned[(g - x) % NP], mixed)
        outs.append(pltpu.roll(mixed, NZ - LP * x, 1) if x else mixed)
    return outs


def kernel(
    cost_ref, pore_ref, heat_ref, dil_ref, cond_ref, resid_ref, pos_ref, wgt_ref,
    out_ref, grad_ref,
    saved, pack, gath, raw, meta, meta_in, state, ysend, yrecv, coef, crep, prep_pore, ypore, ycol, prow, pcol,
    right, gacc, gsum, gpack, gred, outst,
    load_sem, gsend, grecv, ssend, srecv, msem, hsend, hrecv, psend, precv, osend, orecv, rsend, rrecv,
):
    obs, gx, gy = lax.axis_index("obs"), lax.axis_index("gx"), lax.axis_index("gy")
    lobs, lgx = role(obs, gx)
    stays = jnp.logical_and(lobs == obs, lgx == gx)
    moves = jnp.logical_not(stays)
    zh, yy = obs // 2, gx // 2
    ngx, ngy = lax.axis_size("gx"), lax.axis_size("gy")

    lane = lax.broadcasted_iota(jnp.int32, (8, NZ), 1)
    sub = lax.broadcasted_iota(jnp.int32, (8, NZ), 0)
    lane_group = lane // LP
    first_lane, last_lane = lane == 0, lane == NZ - 1

    exists = (lgx > 0, lgx < ngx - 1, gy > 0, gy < ngy - 1)
    xm = role(lobs, jnp.maximum(lgx - 1, 0))
    xp = role(lobs, jnp.minimum(lgx + 1, ngx - 1))
    near = (
        (xm[0], xm[1], gy),
        (xp[0], xp[1], gy),
        (obs, gx, jnp.maximum(gy - 1, 0)),
        (obs, gx, jnp.minimum(gy + 1, ngy - 1)),
    )
    partner = (lobs, lgx, gy)

    fields = (pore_ref, heat_ref, dil_ref, cond_ref)

    def load(n, f):
        return pltpu.make_async_copy(fields[f].at[n], saved.at[n, f], load_sem.at[n, f])

    for n in range(NS - 1, -1, -1):
        for f in range(4):
            load(n, f).start()

    zero = jnp.zeros((8, NZ), F32)
    for st in range(ST):
        for slot in range(2):
            for row in (0, NX + 1):
                state[st, slot, row] = jnp.zeros((ROWS, NZ), F32)
    yrecv[...] = jnp.zeros(yrecv.shape, F32)
    prow[...] = jnp.zeros(prow.shape, F32)
    pcol[...] = jnp.zeros(pcol.shape, F32)

    barrier = pltpu.get_barrier_semaphore()
    for zz in range(4):
        for core in range(2):
            for low in range(2):
                there = (2 * zz + core, 2 * yy + low, gy)

                @pl.when(jnp.logical_or(there[0] != obs, there[1] != gx))
                def _(there=there):
                    pl.semaphore_signal(barrier, inc=1, device_id=there, device_id_type=MESH)

    for k in range(4):

        @pl.when(exists[k])
        def _(k=k):
            pl.semaphore_signal(barrier, inc=1, device_id=near[k], device_id_type=MESH)

    count = 15
    for k in range(4):
        count = count + exists[k].astype(jnp.int32)
    pl.semaphore_wait(barrier, count)

    srow = sub // NQ
    squarter = sub % NQ
    for st in range(ST):
        for n in range(NS):
            tile = zero
            for o in range(SO):
                k = st * SO + o
                tile = jnp.where(srow == o, jnp.broadcast_to(resid_ref[n, k : k + 1, :], (8, NZ)), tile)
            meta[st, n] = tile
        pos = jnp.zeros((8, NZ), jnp.int32)
        wgt = jnp.zeros((8, NZ), jnp.int32)
        for o in range(SO):
            pos = jnp.where(srow == o, pos_ref[st * SO + o], pos)
            wgt = jnp.where(srow == o, wgt_ref[st * SO + o], wgt)
        meta[st, 3] = pos.astype(F32)
        meta[st, 4] = wgt.astype(F32)

    def gather_copy(n, target):
        return pltpu.make_async_remote_copy(
            src_ref=pack.at[n],
            dst_ref=gath.at[n, obs],
            send_sem=gsend.at[n, target],
            recv_sem=grecv.at[n, obs],
            device_id=(2 * (target // 2) + gx % 2, 2 * yy + target % 2, gy),
            device_id_type=MESH,
        )

    def is_me(target):
        return jnp.logical_and(stays, lobs == target)

    def send_saved(n):
        for f in range(4):
            load(n, f).wait()
        for f in range(4):
            for h in range(2):
                packed = saved_tile(n, f, 0, h)
                for x in range(1, NX):
                    packed = jnp.where(
                        lane_group == x, pltpu.roll(saved_tile(n, f, x, h), LP * x, 1), packed
                    )
                pack[n, pl.ds((f * 2 + h) * 8, 8), :] = packed

                @pl.when(stays)
                def _(packed=packed, f=f, h=h):
                    gath[n, obs, pl.ds((f * 2 + h) * 8, 8), :] = packed

        for target in range(NP):

            @pl.when(jnp.logical_not(is_me(target)))
            def _(target=target):
                gather_copy(n, target).start()

    def saved_tile(n, f, x, h):
        piece = saved[n, f, x, pl.ds(h * 8, 8), :]
        return jnp.concatenate([piece, jnp.zeros((8, NZ - LP), F32)], axis=1)

    def swap_in(k):
        return pltpu.make_async_remote_copy(
            src_ref=cost_ref.at[k // NO, k % NO],
            dst_ref=raw.at[:, pl.ds(k * NY, NY), :],
            send_sem=ssend.at[k],
            recv_sem=srecv.at[k],
            device_id=partner,
            device_id_type=MESH,
        )

    def keep_in(k):
        return pltpu.make_async_copy(
            cost_ref.at[k // NO, k % NO], raw.at[:, pl.ds(k * NY, NY), :], srecv.at[k]
        )

    def send_meta():
        return pltpu.make_async_remote_copy(
            src_ref=meta, dst_ref=meta_in, send_sem=msem.at[0], recv_sem=msem.at[1], device_id=partner, device_id_type=MESH
        )

    def streams_obs(st):
        return [f * NO + st * SO + o for f in range(2) for o in range(SO)]

    send_saved(NS - 1)

    @pl.when(moves)
    def _():
        send_meta().start()
        for st in range(ST):
            for k in streams_obs(st):
                swap_in(k).start()

    @pl.when(stays)
    def _():
        for st in range(ST):
            for k in streams_obs(st):
                keep_in(k).start()
        meta_in[...] = meta[...]

    def halo(st, slot, k):
        if k == 0:
            src, dst = state.at[st, slot, 1], state.at[st, slot, NX + 1]
        elif k == 1:
            src, dst = state.at[st, slot, NX], state.at[st, slot, 0]
        elif k == 2:
            src, dst = ysend.at[st, slot, 0], yrecv.at[st, slot, 1]
        else:
            src, dst = ysend.at[st, slot, 1], yrecv.at[st, slot, 0]
        return pltpu.make_async_remote_copy(
            src_ref=src,
            dst_ref=dst,
            send_sem=hsend.at[st, slot, k],
            recv_sem=hrecv.at[st, slot, k ^ 1],
            device_id=near[k],
            device_id_type=MESH,
        )

    def start_halos(st, slot):
        for k in range(4):

            @pl.when(exists[k])
            def _(k=k):
                halo(st, slot, k).start()

    def wait_halos(st, slot):
        for k in range(4):

            @pl.when(exists[k])
            def _(k=k):
                halo(st, slot, k ^ 1).wait_recv()
                halo(st, slot, k).wait_send()

    def y_message(st, slot, xg, firsts, lasts):
        low, high = firsts[0], pltpu.roll(lasts[0], (9 - NQ) % 8, 0)
        for i in range(1, NQ):
            low = jnp.where(squarter == i, pltpu.roll(firsts[i], i, 0), low)
            turned = lasts[i] if i == NQ - 1 else pltpu.roll(lasts[i], (9 + i - NQ) % 8, 0)
            high = jnp.where(squarter == i, turned, high)
        ysend[st, slot, 0, pl.ds(xg * 8, 8), :] = low
        ysend[st, slot, 1, pl.ds(xg * 8, 8), :] = high

    def set_up(st):
        @pl.when(moves)
        def _():
            for k in streams_obs(st):
                swap_in(k).wait()

        @pl.when(stays)
        def _():
            for k in streams_obs(st):
                keep_in(k).wait()

        def first_rows(xg, _):
            firsts, lasts = [], []
            for g in range(NG):
                x = xg + g * XG
                for f in range(2):
                    start = (f * NO + st * SO) * NY
                    tiles = [raw[x, pl.ds(start + j, 8, stride=NJ), :] for j in range(NJ)]
                    for j in range(NJ):
                        state[st, 0, x + 1, pl.ds((f * NJ + j) * 8, 8), :] = tiles[j]
                    firsts.append(tiles[0])
                    lasts.append(tiles[-1])
            y_message(st, 0, xg, firsts, lasts)
            return 0

        lax.fori_loop(0, XG, first_rows, 0)
        start_halos(st, 0)

    def around(tiles, up, down, before, after):
        sums = []
        for j in range(NJ):
            here = tiles[j]
            total = up[j] + down[j]
            total = total + (tiles[j - 1] if j else before) + (tiles[j + 1] if j < NJ - 1 else after)
            deep = jnp.where(first_lane, 0.0, pltpu.roll(here, 1, 1))
            shallow = jnp.where(last_lane, 0.0, pltpu.roll(here, NZ - 1, 1))
            sums.append(total + deep + shallow)
        return sums

    def ends_of(tiles, low, high):
        before = jnp.where(squarter == 0, low, pltpu.roll(tiles[-1], 1, 0))
        after = jnp.where(squarter == NQ - 1, high, pltpu.roll(tiles[0], 7, 0))
        return before, after

    def relax_rows(st, slot, n, xg):
        low = yrecv[st, slot, 0, pl.ds(xg * 8, 8), :]
        high = yrecv[st, slot, 1, pl.ds(xg * 8, 8), :]
        firsts, lasts = [], []
        for g in range(NG):
            x = xg + g * XG
            tiles, sums = [], []
            for f in range(2):
                here, up, down = (
                    [state[st, slot, x + dx, pl.ds((f * NJ + j) * 8, 8), :] for j in range(NJ)] for dx in (1, 0, 2)
                )
                i = 2 * g + f
                low_i = pltpu.roll(low, 8 - i, 0) if i else low
                high_i = pltpu.roll(high, NQ - 1 - i, 0) if i < NQ - 1 else high
                tiles.append(here)
                sums.append(around(here, up, down, *ends_of(here, low_i, high_i)))
            new = [[], []]
            for j in range(NJ):
                at = pl.ds(j * 8, 8)
                at_t = pl.ds((NJ + j) * 8, 8)
                new_p = right[st, x, at, :] + coef[n, AP, x, at, :] * sums[0][j] + coef[n, BP, x, at, :] * tiles[1][j]
                new_t = right[st, x, at_t, :] + coef[n, AT, x, at, :] * sums[1][j] + coef[n, BT, x, at, :] * new_p
                state[st, 1 - slot, x + 1, at, :] = new_p
                state[st, 1 - slot, x + 1, at_t, :] = new_t
                new[0].append(new_p)
                new[1].append(new_t)
            for f in range(2):
                firsts.append(new[f][0])
                lasts.append(new[f][-1])
        y_message(st, 1 - slot, xg, firsts, lasts)

    base_cell = (lgx * NX) * (ngy * NY) + gy * NY

    def pore_halo(n, k):
        if k == 0:
            src, dst = ypore.at[n, pl.ds(0, NY)], prow.at[n, 1]
        elif k == 1:
            src, dst = ypore.at[n, pl.ds((NX - 1) * NY, NY)], prow.at[n, 0]
        elif k == 2:
            src, dst = ycol.at[n, 0], pcol.at[n, 1]
        else:
            src, dst = ycol.at[n, 1], pcol.at[n, 0]
        return pltpu.make_async_remote_copy(
            src_ref=src,
            dst_ref=dst,
            send_sem=psend.at[n, k],
            recv_sem=precv.at[n, k ^ 1],
            device_id=near[k],
            device_id_type=MESH,
        )

    def repeat(ref, lead, h, value):
        for o in range(SO):
            ref[(*lead, pl.ds(o * NY + h * 8, 8), slice(None))] = value

    def prepare(n):
        for d in range(NP):

            @pl.when(jnp.logical_not(jnp.logical_and(stays, obs == d)))
            def _(d=d):
                pltpu.make_async_remote_copy(
                    src_ref=pack.at[n],
                    dst_ref=gath.at[n, d],
                    send_sem=gsend.at[n, d],
                    recv_sem=grecv.at[n, d],
                    device_id=partner,
                    device_id_type=MESH,
                ).wait_recv()

        for h in range(2):
            whole = [
                regroup([gath[n, d, pl.ds((f * 2 + h) * 8, 8), :] for d in range(NP)], lane_group) for f in range(4)
            ]
            for x in range(NX):
                pore, heat, dil, perm = (whole[f][x] for f in range(4))
                store_p = jnp.exp(dil)
                store_t = jnp.exp(0.5 * heat)
                coupling = 0.2 * jnp.tanh(pore)
                inv_p = 1.0 / (store_p + 6.0 * perm)
                inv_t = 1.0 / (store_t + 12.0)
                repeat(crep, (AP, x), h, perm * inv_p)
                repeat(crep, (BP, x), h, coupling * inv_p)
                repeat(crep, (AT, x), h, 2.0 * inv_t)
                repeat(crep, (BT, x), h, coupling * inv_t)
                repeat(crep, (RPC, x), h, store_p * inv_p)
                repeat(crep, (IP, x), h, inv_p)
                repeat(crep, (RTC, x), h, store_t * inv_t)
                repeat(crep, (KK, x), h, perm)
                repeat(prep_pore, (x + 1,), h, pore)
                ypore[n, pl.ds(x * NY + h * 8, 8), :] = pore
        for side, y in ((0, 0), (1, NY - 1)):
            ycol[n, side] = ypore[n, pl.ds(y, NX, stride=NY), :]
        for k in range(4):

            @pl.when(exists[k])
            def _(k=k):
                pore_halo(n, k).start()

        def spread(x, _):
            for c in range(8):
                for j in range(NJ):
                    coef[n, c, x, pl.ds(j * 8, 8), :] = crep[c, x, pl.ds(j, 8, stride=NJ), :]
            return 0

        lax.fori_loop(0, NX, spread, 0)

    def right_sides(st, n):
        source = meta_in[st, n]
        cell = meta_in[st, 3] - (NJ * squarter + base_cell).astype(F32)

        def row(x, _):
            for j in range(NJ):
                at = pl.ds(j * 8, 8)
                at_t = pl.ds((NJ + j) * 8, 8)
                mine = cell == (x * (ngy * NY) + j).astype(F32)
                term = jnp.where(mine, source, 0.0)
                right[st, x, at, :] = (
                    coef[n, RPC, x, at, :] * state[st, 0, x + 1, at, :] + coef[n, IP, x, at, :] * term
                )
                right[st, x, at_t, :] = coef[n, RTC, x, at, :] * state[st, 0, x + 1, at_t, :]
            return 0

        lax.fori_loop(0, NX, row, 0)

    def gradient_factor(n):
        for k in range(4):

            @pl.when(exists[k])
            def _(k=k):
                pore_halo(n, k ^ 1).wait_recv()
                pore_halo(n, k).wait_send()

        for side, row in ((0, 0), (1, NX + 1)):
            for h in range(2):
                repeat(prep_pore, (row,), h, prow[n, side, pl.ds(h * 8, 8), :])

        def row(x, _):
            tiles, up, down = (
                [prep_pore[x + dx, pl.ds(j, 8, stride=NJ), :] for j in range(NJ)] for dx in (1, 0, 2)
            )
            low = jnp.broadcast_to(pcol[n, 0, pl.ds(x, 1), :], (8, NZ))
            high = jnp.broadcast_to(pcol[n, 1, pl.ds(x, 1), :], (8, NZ))
            sums = around(tiles, up, down, *ends_of(tiles, low, high))
            for j in range(NJ):
                at = pl.ds(j * 8, 8)
                coef[n, KK, x, at, :] = coef[n, KK, x, at, :] * (sums[j] - 6.0 * tiles[j])
            return 0

        lax.fori_loop(0, NX, row, 0)

    def add_gradient(st, n):
        weight = meta_in[st, 4]

        def row(x, _):
            for j in range(NJ):
                at = pl.ds(j * 8, 8)
                gacc[x, at, :] += coef[n, KK, x, at, :] * (weight * state[st, 0, x + 1, at, :])
            return 0

        lax.fori_loop(0, NX, row, 0)

    def swap_out(k):
        return pltpu.make_async_remote_copy(
            src_ref=outst.at[:, pl.ds(k * NY, NY), :],
            dst_ref=out_ref.at[k // NO, k % NO],
            send_sem=osend.at[k],
            recv_sem=orecv.at[k],
            device_id=partner,
            device_id_type=MESH,
        )

    def keep_out(k):
        return pltpu.make_async_copy(
            outst.at[:, pl.ds(k * NY, NY), :], out_ref.at[k // NO, k % NO], orecv.at[k]
        )

    def finish(st):
        def row(x, _):
            for f in range(2):
                for j in range(NJ):
                    outst[x, pl.ds((f * NO + st * SO) * NY + j, 8, stride=NJ), :] = state[
                        st, 0, x + 1, pl.ds((f * NJ + j) * 8, 8), :
                    ]
            return 0

        lax.fori_loop(0, NX, row, 0)

        @pl.when(moves)
        def _():
            for k in streams_obs(st):
                swap_out(k).start()

        @pl.when(stays)
        def _():
            for k in streams_obs(st):
                keep_out(k).start()

    def iterate(st, k):
        n, slot = NS - 1 - k // ITERS, k % 2
        if k % ITERS == 0:
            right_sides(st, n)
        wait_halos(st, slot)

        def rows(xg, _):
            relax_rows(st, slot, n, xg)
            return 0

        lax.fori_loop(0, XG, rows, 0, unroll=UNROLL)
        if k < NS * ITERS - 1:
            start_halos(st, 1 - slot)
        else:
            finish(st)
        if k % ITERS == ITERS - 1:
            add_gradient(st, n)

    gacc[...] = jnp.zeros(gacc.shape, F32)
    set_up(0)

    @pl.when(moves)
    def _():
        send_meta().wait()

    prepare(NS - 1)
    for k in range(NS * ITERS + ST - 1):
        n = NS - 1 - k // ITERS
        if k % ITERS == 0 and 0 < k < NS * ITERS:
            prepare(n)
        if k % ITERS == ITERS - 1:
            gradient_factor(n)
        if k < ST:
            if k > 0:
                set_up(k)
        for st in range(ST):
            if 0 <= k - st < NS * ITERS:
                iterate(st, k - st)
        if k < NS - 1:
            send_saved(NS - 2 - k)

    for x in range(NX):
        for j in range(NJ):
            total = gacc[x, pl.ds(j * 8, 8), :]
            for o in range(1, SO):
                total = total + pltpu.roll(gacc[x, pl.ds(j * 8, 8), :], NQ * o, 0)
            gsum[x, pl.ds(j, 8, stride=NJ), :] = total
    for h in range(2):
        whole = [gsum[x, pl.ds(h * 8, 8), :] for x in range(NX)]
        for d, tile in enumerate(regroup(whole, lane_group)):
            gpack[d, pl.ds(h * 8, 8), :] = tile

            @pl.when(jnp.logical_and(stays, obs == d))
            def _(tile=tile, h=h):
                gred[lobs, pl.ds(h * 8, 8), :] = tile

    def reduce_copy(d):
        return pltpu.make_async_remote_copy(
            src_ref=gpack.at[d],
            dst_ref=gred.at[lobs],
            send_sem=rsend.at[d],
            recv_sem=rrecv.at[lobs],
            device_id=(d, lgx, gy),
            device_id_type=MESH,
        )

    for d in range(NP):

        @pl.when(jnp.logical_not(jnp.logical_and(stays, obs == d)))
        def _(d=d):
            reduce_copy(d).start()

    for d in range(NP):

        @pl.when(jnp.logical_not(is_me(d)))
        def _(d=d):
            pltpu.make_async_remote_copy(
                src_ref=gpack.at[d],
                dst_ref=gred.at[d],
                send_sem=rsend.at[d],
                recv_sem=rrecv.at[d],
                device_id=partner,
                device_id_type=MESH,
            ).wait_recv()

    for h in range(2):
        total = gred[0, pl.ds(h * 8, 8), :]
        for d in range(1, NP):
            total = total + gred[d, pl.ds(h * 8, 8), :]
        for x in range(NX):
            turned = pltpu.roll(total, NZ - LP * x, 1) if x else total
            grad_ref[x, pl.ds(h * 8, 8), :] = turned[:, :LP]

    for d in range(NP):

        @pl.when(jnp.logical_not(jnp.logical_and(stays, obs == d)))
        def _(d=d):
            reduce_copy(d).wait_send()

    for n in range(NS):
        for target in range(NP):

            @pl.when(jnp.logical_not(is_me(target)))
            def _(n=n, target=target):
                gather_copy(n, target).wait_send()

    @pl.when(moves)
    def _():
        for k in range(2 * NO):
            swap_out(k).wait()

    @pl.when(stays)
    def _():
        for k in range(2 * NO):
            keep_out(k).wait()


def local(*args):
    hbm = pl.BlockSpec(memory_space=pl.ANY)
    vmem = pl.BlockSpec(memory_space=pltpu.VMEM)
    smem = pl.BlockSpec(memory_space=pltpu.SMEM)
    dma = pltpu.SemaphoreType.DMA
    return pl.pallas_call(
        kernel,
        out_shape=(
            jax.ShapeDtypeStruct((2, NO, NX, NY, NZ), F32),
            jax.ShapeDtypeStruct((NX, NY, LP), F32),
        ),
        in_specs=[hbm, hbm, hbm, hbm, hbm, vmem, smem, smem],
        out_specs=(hbm, vmem),
        scratch_shapes=[
            pltpu.VMEM((NS, 4, NX, NY, LP), F32),
            pltpu.VMEM((NS, 64, NZ), F32),
            pltpu.VMEM((NS, NP, 64, NZ), F32),
            pltpu.VMEM((NX, 2 * NO * NY, NZ), F32),
            pltpu.VMEM((ST, 5, 8, NZ), F32),
            pltpu.VMEM((ST, 5, 8, NZ), F32),
            pltpu.VMEM((ST, 2, NX + 2, ROWS, NZ), F32),
            pltpu.VMEM((ST, 2, 2, XG * 8, NZ), F32),
            pltpu.VMEM((ST, 2, 2, XG * 8, NZ), F32),
            pltpu.VMEM((NS, 8, NX, NJ * 8, NZ), F32),
            pltpu.VMEM((8, NX, SO * NY, NZ), F32),
            pltpu.VMEM((NX + 2, SO * NY, NZ), F32),
            pltpu.VMEM((NS, NX * NY, NZ), F32),
            pltpu.VMEM((NS, 2, 8, NZ), F32),
            pltpu.VMEM((NS, 2, NY, NZ), F32),
            pltpu.VMEM((NS, 2, 8, NZ), F32),
            pltpu.VMEM((ST, NX, ROWS, NZ), F32),
            pltpu.VMEM((NX, NJ * 8, NZ), F32),
            pltpu.VMEM((NX, 8 * NJ, NZ), F32),
            pltpu.VMEM((NP, NY, NZ), F32),
            pltpu.VMEM((NP, NY, NZ), F32),
            pltpu.VMEM((NX, 2 * NO * NY, NZ), F32),
            dma((NS, 4)),
            dma((NS, NP)),
            dma((NS, NP)),
            dma((2 * NO,)),
            dma((2 * NO,)),
            dma((2,)),
            dma((ST, 2, 4)),
            dma((ST, 2, 4)),
            dma((NS, 4)),
            dma((NS, 4)),
            dma((2 * NO,)),
            dma((2 * NO,)),
            dma((NP,)),
            dma((NP,)),
        ],
        compiler_params=pltpu.CompilerParams(
            collective_id=0, has_side_effects=True, vmem_limit_bytes=48 * 1024 * 1024
        ),
    )(*args)


def solution(mesh):
    return jax.shard_map(
        local,
        mesh=mesh,
        in_specs=(
            P(None, "obs", "gx", "gy", None),
            P(None, "gx", "gy", "obs"),
            P(None, "gx", "gy", "obs"),
            P(None, "gx", "gy", "obs"),
            P(None, "gx", "gy", "obs"),
            P(None, "obs", None),
            P("obs"),
            P("obs"),
        ),
        out_specs=(P(None, "obs", "gx", "gy", None), P("gx", "gy", "obs")),
        check_vma=False,
    )
```

```python
import functools

import jax
import jax.numpy as jnp
from jax import lax
from jax.experimental import pallas as pl
from jax.experimental.pallas import tpu as pltpu
from jax.sharding import PartitionSpec as P

MESH = pl.DeviceIdType.MESH
F32 = jnp.float32
ITERS = 4
UNROLL = 4
NX, NY, NZ = 8, 16, 128
NS = 3
NO = 4
NP = 8
LP = NZ // NP
SO = 2
ST = NO // SO
NQ = 8 // SO
NJ = NY // NQ
NG = NQ // 2
XG = NX // NG
ROWS = 2 * NJ * 8
AP, BP, AT, BT, RPC, IP, RTC, KK = range(8)


def role(obs, gx):
    return 2 * (obs // 2) + gx % 2, 2 * (gx // 2) + obs % 2


def regroup(tiles, lane_group):
    turned = [pltpu.roll(t, LP * d, 1) if d else t for d, t in enumerate(tiles)]
    outs = []
    for x in range(NP):
        mixed = turned[(NP - 1 - x) % NP]
        for g in range(NP - 1):
            mixed = jnp.where(lane_group == g, turned[(g - x) % NP], mixed)
        outs.append(pltpu.roll(mixed, NZ - LP * x, 1) if x else mixed)
    return outs


def kernel(
    cost_ref, pore_ref, heat_ref, dil_ref, cond_ref, resid_ref, pos_ref, wgt_ref,
    out_ref, grad_ref,
    saved, pack, gath, raw, meta, meta_in, state, ysend, yrecv, coef, crep, prep_pore, ypore, ycol, prow, pcol,
    right, gacc, gsum, gpack, gred, outst,
    load_sem, gsend, grecv, ssend, srecv, msem, hsend, hrecv, psend, precv, osend, orecv, rsend, rrecv,
):
    obs, gx, gy = lax.axis_index("obs"), lax.axis_index("gx"), lax.axis_index("gy")
    lobs, lgx = role(obs, gx)
    stays = jnp.logical_and(lobs == obs, lgx == gx)
    moves = jnp.logical_not(stays)
    zh, yy = obs // 2, gx // 2
    ngx, ngy = lax.axis_size("gx"), lax.axis_size("gy")

    lane = lax.broadcasted_iota(jnp.int32, (8, NZ), 1)
    sub = lax.broadcasted_iota(jnp.int32, (8, NZ), 0)
    lane_group = lane // LP
    first_lane, last_lane = lane == 0, lane == NZ - 1

    exists = (lgx > 0, lgx < ngx - 1, gy > 0, gy < ngy - 1)
    xm = role(lobs, jnp.maximum(lgx - 1, 0))
    xp = role(lobs, jnp.minimum(lgx + 1, ngx - 1))
    near = (
        (xm[0], xm[1], gy),
        (xp[0], xp[1], gy),
        (obs, gx, jnp.maximum(gy - 1, 0)),
        (obs, gx, jnp.minimum(gy + 1, ngy - 1)),
    )
    partner = (lobs, lgx, gy)

    fields = (pore_ref, heat_ref, dil_ref, cond_ref)

    def load(n, f):
        return pltpu.make_async_copy(fields[f].at[n], saved.at[n, f], load_sem.at[n, f])

    for n in range(NS - 1, -1, -1):
        for f in range(4):
            load(n, f).start()

    zero = jnp.zeros((8, NZ), F32)
    for st in range(ST):
        for slot in range(2):
            for row in (0, NX + 1):
                state[st, slot, row] = jnp.zeros((ROWS, NZ), F32)
    yrecv[...] = jnp.zeros(yrecv.shape, F32)
    prow[...] = jnp.zeros(prow.shape, F32)
    pcol[...] = jnp.zeros(pcol.shape, F32)

    barrier = pltpu.get_barrier_semaphore()
    for zz in range(4):
        for core in range(2):
            for low in range(2):
                there = (2 * zz + core, 2 * yy + low, gy)

                @pl.when(jnp.logical_or(there[0] != obs, there[1] != gx))
                def _(there=there):
                    pl.semaphore_signal(barrier, inc=1, device_id=there, device_id_type=MESH)

    for k in range(4):

        @pl.when(exists[k])
        def _(k=k):
            pl.semaphore_signal(barrier, inc=1, device_id=near[k], device_id_type=MESH)

    count = 15
    for k in range(4):
        count = count + exists[k].astype(jnp.int32)
    pl.semaphore_wait(barrier, count)

    srow = sub // NQ
    squarter = sub % NQ
    for st in range(ST):
        for n in range(NS):
            tile = zero
            for o in range(SO):
                k = st * SO + o
                tile = jnp.where(srow == o, jnp.broadcast_to(resid_ref[n, k : k + 1, :], (8, NZ)), tile)
            meta[st, n] = tile
        pos = jnp.zeros((8, NZ), jnp.int32)
        wgt = jnp.zeros((8, NZ), jnp.int32)
        for o in range(SO):
            pos = jnp.where(srow == o, pos_ref[st * SO + o], pos)
            wgt = jnp.where(srow == o, wgt_ref[st * SO + o], wgt)
        meta[st, 3] = pos.astype(F32)
        meta[st, 4] = wgt.astype(F32)

    def gather_copy(n, target):
        return pltpu.make_async_remote_copy(
            src_ref=pack.at[n],
            dst_ref=gath.at[n, obs],
            send_sem=gsend.at[n, target],
            recv_sem=grecv.at[n, obs],
            device_id=(2 * (target // 2) + gx % 2, 2 * yy + target % 2, gy),
            device_id_type=MESH,
        )

    def is_me(target):
        return jnp.logical_and(stays, lobs == target)

    def send_saved(n):
        for f in range(4):
            load(n, f).wait()
        for f in range(4):
            for h in range(2):
                packed = saved_tile(n, f, 0, h)
                for x in range(1, NX):
                    packed = jnp.where(
                        lane_group == x, pltpu.roll(saved_tile(n, f, x, h), LP * x, 1), packed
                    )
                pack[n, pl.ds((f * 2 + h) * 8, 8), :] = packed

                @pl.when(stays)
                def _(packed=packed, f=f, h=h):
                    gath[n, obs, pl.ds((f * 2 + h) * 8, 8), :] = packed

        for target in range(NP):

            @pl.when(jnp.logical_not(is_me(target)))
            def _(target=target):
                gather_copy(n, target).start()

    def saved_tile(n, f, x, h):
        piece = saved[n, f, x, pl.ds(h * 8, 8), :]
        return jnp.concatenate([piece, jnp.zeros((8, NZ - LP), F32)], axis=1)

    def swap_in(k):
        return pltpu.make_async_remote_copy(
            src_ref=cost_ref.at[k // NO, k % NO],
            dst_ref=raw.at[:, pl.ds(k * NY, NY), :],
            send_sem=ssend.at[k],
            recv_sem=srecv.at[k],
            device_id=partner,
            device_id_type=MESH,
        )

    def keep_in(k):
        return pltpu.make_async_copy(
            cost_ref.at[k // NO, k % NO], raw.at[:, pl.ds(k * NY, NY), :], srecv.at[k]
        )

    def send_meta():
        return pltpu.make_async_remote_copy(
            src_ref=meta, dst_ref=meta_in, send_sem=msem.at[0], recv_sem=msem.at[1], device_id=partner, device_id_type=MESH
        )

    def streams_obs(st):
        return [f * NO + st * SO + o for f in range(2) for o in range(SO)]

    send_saved(NS - 1)

    @pl.when(moves)
    def _():
        send_meta().start()
        for st in range(ST):
            for k in streams_obs(st):
                swap_in(k).start()

    @pl.when(stays)
    def _():
        for st in range(ST):
            for k in streams_obs(st):
                keep_in(k).start()
        meta_in[...] = meta[...]

    def halo(st, slot, k):
        if k == 0:
            src, dst = state.at[st, slot, 1], state.at[st, slot, NX + 1]
        elif k == 1:
            src, dst = state.at[st, slot, NX], state.at[st, slot, 0]
        elif k == 2:
            src, dst = ysend.at[st, slot, 0], yrecv.at[st, slot, 1]
        else:
            src, dst = ysend.at[st, slot, 1], yrecv.at[st, slot, 0]
        return pltpu.make_async_remote_copy(
            src_ref=src,
            dst_ref=dst,
            send_sem=hsend.at[st, slot, k],
            recv_sem=hrecv.at[st, slot, k ^ 1],
            device_id=near[k],
            device_id_type=MESH,
        )

    def start_halos(st, slot):
        for k in range(4):

            @pl.when(exists[k])
            def _(k=k):
                halo(st, slot, k).start()

    def wait_halos(st, slot):
        for k in range(4):

            @pl.when(exists[k])
            def _(k=k):
                halo(st, slot, k ^ 1).wait_recv()
                halo(st, slot, k).wait_send()

    def y_message(st, slot, xg, firsts, lasts):
        low, high = firsts[0], pltpu.roll(lasts[0], (9 - NQ) % 8, 0)
        for i in range(1, NQ):
            low = jnp.where(squarter == i, pltpu.roll(firsts[i], i, 0), low)
            turned = lasts[i] if i == NQ - 1 else pltpu.roll(lasts[i], (9 + i - NQ) % 8, 0)
            high = jnp.where(squarter == i, turned, high)
        ysend[st, slot, 0, pl.ds(xg * 8, 8), :] = low
        ysend[st, slot, 1, pl.ds(xg * 8, 8), :] = high

    def set_up(st):
        @pl.when(moves)
        def _():
            for k in streams_obs(st):
                swap_in(k).wait()

        @pl.when(stays)
        def _():
            for k in streams_obs(st):
                keep_in(k).wait()

        def first_rows(xg, _):
            firsts, lasts = [], []
            for g in range(NG):
                x = xg + g * XG
                for f in range(2):
                    start = (f * NO + st * SO) * NY
                    tiles = [raw[x, pl.ds(start + j, 8, stride=NJ), :] for j in range(NJ)]
                    for j in range(NJ):
                        state[st, 0, x + 1, pl.ds((f * NJ + j) * 8, 8), :] = tiles[j]
                    firsts.append(tiles[0])
                    lasts.append(tiles[-1])
            y_message(st, 0, xg, firsts, lasts)
            return 0

        lax.fori_loop(0, XG, first_rows, 0)
        start_halos(st, 0)

    def around(tiles, up, down, before, after):
        sums = []
        for j in range(NJ):
            here = tiles[j]
            total = up[j] + down[j]
            total = total + (tiles[j - 1] if j else before) + (tiles[j + 1] if j < NJ - 1 else after)
            deep = jnp.where(first_lane, 0.0, pltpu.roll(here, 1, 1))
            shallow = jnp.where(last_lane, 0.0, pltpu.roll(here, NZ - 1, 1))
            sums.append(total + deep + shallow)
        return sums

    def ends_of(tiles, low, high):
        before = jnp.where(squarter == 0, low, pltpu.roll(tiles[-1], 1, 0))
        after = jnp.where(squarter == NQ - 1, high, pltpu.roll(tiles[0], 7, 0))
        return before, after

    def relax_rows(st, slot, n, xg):
        low = yrecv[st, slot, 0, pl.ds(xg * 8, 8), :]
        high = yrecv[st, slot, 1, pl.ds(xg * 8, 8), :]
        firsts, lasts = [], []
        for g in range(NG):
            x = xg + g * XG
            tiles, sums = [], []
            for f in range(2):
                here, up, down = (
                    [state[st, slot, x + dx, pl.ds((f * NJ + j) * 8, 8), :] for j in range(NJ)] for dx in (1, 0, 2)
                )
                i = 2 * g + f
                low_i = pltpu.roll(low, 8 - i, 0) if i else low
                high_i = pltpu.roll(high, NQ - 1 - i, 0) if i < NQ - 1 else high
                tiles.append(here)
                sums.append(around(here, up, down, *ends_of(here, low_i, high_i)))
            new = [[], []]
            for j in range(NJ):
                at = pl.ds(j * 8, 8)
                at_t = pl.ds((NJ + j) * 8, 8)
                new_p = right[st, x, at, :] + coef[n, AP, x, at, :] * sums[0][j] + coef[n, BP, x, at, :] * tiles[1][j]
                new_t = right[st, x, at_t, :] + coef[n, AT, x, at, :] * sums[1][j] + coef[n, BT, x, at, :] * new_p
                state[st, 1 - slot, x + 1, at, :] = new_p
                state[st, 1 - slot, x + 1, at_t, :] = new_t
                new[0].append(new_p)
                new[1].append(new_t)
            for f in range(2):
                firsts.append(new[f][0])
                lasts.append(new[f][-1])
        y_message(st, 1 - slot, xg, firsts, lasts)

    base_cell = (lgx * NX) * (ngy * NY) + gy * NY

    def pore_halo(n, k):
        if k == 0:
            src, dst = ypore.at[n, pl.ds(0, NY)], prow.at[n, 1]
        elif k == 1:
            src, dst = ypore.at[n, pl.ds((NX - 1) * NY, NY)], prow.at[n, 0]
        elif k == 2:
            src, dst = ycol.at[n, 0], pcol.at[n, 1]
        else:
            src, dst = ycol.at[n, 1], pcol.at[n, 0]
        return pltpu.make_async_remote_copy(
            src_ref=src,
            dst_ref=dst,
            send_sem=psend.at[n, k],
            recv_sem=precv.at[n, k ^ 1],
            device_id=near[k],
            device_id_type=MESH,
        )

    def repeat(ref, lead, h, value):
        for o in range(SO):
            ref[(*lead, pl.ds(o * NY + h * 8, 8), slice(None))] = value

    def prepare(n):
        for d in range(NP):

            @pl.when(jnp.logical_not(jnp.logical_and(stays, obs == d)))
            def _(d=d):
                pltpu.make_async_remote_copy(
                    src_ref=pack.at[n],
                    dst_ref=gath.at[n, d],
                    send_sem=gsend.at[n, d],
                    recv_sem=grecv.at[n, d],
                    device_id=partner,
                    device_id_type=MESH,
                ).wait_recv()

        for h in range(2):
            whole = [
                regroup([gath[n, d, pl.ds((f * 2 + h) * 8, 8), :] for d in range(NP)], lane_group) for f in range(4)
            ]
            for x in range(NX):
                pore, heat, dil, perm = (whole[f][x] for f in range(4))
                store_p = jnp.exp(dil)
                store_t = jnp.exp(0.5 * heat)
                coupling = 0.2 * jnp.tanh(pore)
                inv_p = 1.0 / (store_p + 6.0 * perm)
                inv_t = 1.0 / (store_t + 12.0)
                repeat(crep, (AP, x), h, perm * inv_p)
                repeat(crep, (BP, x), h, coupling * inv_p)
                repeat(crep, (AT, x), h, 2.0 * inv_t)
                repeat(crep, (BT, x), h, coupling * inv_t)
                repeat(crep, (RPC, x), h, store_p * inv_p)
                repeat(crep, (IP, x), h, inv_p)
                repeat(crep, (RTC, x), h, store_t * inv_t)
                repeat(crep, (KK, x), h, perm)
                repeat(prep_pore, (x + 1,), h, pore)
                ypore[n, pl.ds(x * NY + h * 8, 8), :] = pore
        for side, y in ((0, 0), (1, NY - 1)):
            ycol[n, side] = ypore[n, pl.ds(y, NX, stride=NY), :]
        for k in range(4):

            @pl.when(exists[k])
            def _(k=k):
                pore_halo(n, k).start()

        def spread(x, _):
            for c in range(8):
                for j in range(NJ):
                    coef[n, c, x, pl.ds(j * 8, 8), :] = crep[c, x, pl.ds(j, 8, stride=NJ), :]
            return 0

        lax.fori_loop(0, NX, spread, 0)

    def right_sides(st, n):
        source = meta_in[st, n]
        cell = meta_in[st, 3] - (NJ * squarter + base_cell).astype(F32)

        def row(x, _):
            for j in range(NJ):
                at = pl.ds(j * 8, 8)
                at_t = pl.ds((NJ + j) * 8, 8)
                mine = cell == (x * (ngy * NY) + j).astype(F32)
                term = jnp.where(mine, source, 0.0)
                right[st, x, at, :] = (
                    coef[n, RPC, x, at, :] * state[st, 0, x + 1, at, :] + coef[n, IP, x, at, :] * term
                )
                right[st, x, at_t, :] = coef[n, RTC, x, at, :] * state[st, 0, x + 1, at_t, :]
            return 0

        lax.fori_loop(0, NX, row, 0)

    def gradient_factor(n):
        for k in range(4):

            @pl.when(exists[k])
            def _(k=k):
                pore_halo(n, k ^ 1).wait_recv()
                pore_halo(n, k).wait_send()

        for side, row in ((0, 0), (1, NX + 1)):
            for h in range(2):
                repeat(prep_pore, (row,), h, prow[n, side, pl.ds(h * 8, 8), :])

        def row(x, _):
            tiles, up, down = (
                [prep_pore[x + dx, pl.ds(j, 8, stride=NJ), :] for j in range(NJ)] for dx in (1, 0, 2)
            )
            low = jnp.broadcast_to(pcol[n, 0, pl.ds(x, 1), :], (8, NZ))
            high = jnp.broadcast_to(pcol[n, 1, pl.ds(x, 1), :], (8, NZ))
            sums = around(tiles, up, down, *ends_of(tiles, low, high))
            for j in range(NJ):
                at = pl.ds(j * 8, 8)
                coef[n, KK, x, at, :] = coef[n, KK, x, at, :] * (sums[j] - 6.0 * tiles[j])
            return 0

        lax.fori_loop(0, NX, row, 0)

    def add_gradient(st, n):
        weight = meta_in[st, 4]

        def row(x, _):
            for j in range(NJ):
                at = pl.ds(j * 8, 8)
                gacc[x, at, :] += coef[n, KK, x, at, :] * (weight * state[st, 0, x + 1, at, :])
            return 0

        lax.fori_loop(0, NX, row, 0)

    def swap_out(k):
        return pltpu.make_async_remote_copy(
            src_ref=outst.at[:, pl.ds(k * NY, NY), :],
            dst_ref=out_ref.at[k // NO, k % NO],
            send_sem=osend.at[k],
            recv_sem=orecv.at[k],
            device_id=partner,
            device_id_type=MESH,
        )

    def keep_out(k):
        return pltpu.make_async_copy(
            outst.at[:, pl.ds(k * NY, NY), :], out_ref.at[k // NO, k % NO], orecv.at[k]
        )

    def finish(st):
        def row(x, _):
            for f in range(2):
                for j in range(NJ):
                    outst[x, pl.ds((f * NO + st * SO) * NY + j, 8, stride=NJ), :] = state[
                        st, 0, x + 1, pl.ds((f * NJ + j) * 8, 8), :
                    ]
            return 0

        lax.fori_loop(0, NX, row, 0)

        @pl.when(moves)
        def _():
            for k in streams_obs(st):
                swap_out(k).start()

        @pl.when(stays)
        def _():
            for k in streams_obs(st):
                keep_out(k).start()

    def iterate(st, k):
        n, slot = NS - 1 - k // ITERS, k % 2
        if k % ITERS == 0:
            right_sides(st, n)
        wait_halos(st, slot)

        def rows(xg, _):
            relax_rows(st, slot, n, xg)
            return 0

        lax.fori_loop(0, XG, rows, 0, unroll=UNROLL)
        if k < NS * ITERS - 1:
            start_halos(st, 1 - slot)
        else:
            finish(st)
        if k % ITERS == ITERS - 1:
            add_gradient(st, n)

    gacc[...] = jnp.zeros(gacc.shape, F32)
    set_up(0)

    @pl.when(moves)
    def _():
        send_meta().wait()

    prepare(NS - 1)
    for k in range(NS * ITERS + ST - 1):
        n = NS - 1 - k // ITERS
        if k % ITERS == 0 and 0 < k < NS * ITERS:
            prepare(n)
        if k % ITERS == ITERS - 1:
            gradient_factor(n)
        if k < ST:
            if k > 0:
                set_up(k)
        for st in range(ST):
            if 0 <= k - st < NS * ITERS:
                iterate(st, k - st)
        if k < NS - 1:
            send_saved(NS - 2 - k)

    for x in range(NX):
        for j in range(NJ):
            total = gacc[x, pl.ds(j * 8, 8), :]
            for o in range(1, SO):
                total = total + pltpu.roll(gacc[x, pl.ds(j * 8, 8), :], NQ * o, 0)
            gsum[x, pl.ds(j, 8, stride=NJ), :] = total
    for h in range(2):
        whole = [gsum[x, pl.ds(h * 8, 8), :] for x in range(NX)]
        for d, tile in enumerate(regroup(whole, lane_group)):
            gpack[d, pl.ds(h * 8, 8), :] = tile

            @pl.when(jnp.logical_and(stays, obs == d))
            def _(tile=tile, h=h):
                gred[lobs, pl.ds(h * 8, 8), :] = tile

    def reduce_copy(d):
        return pltpu.make_async_remote_copy(
            src_ref=gpack.at[d],
            dst_ref=gred.at[lobs],
            send_sem=rsend.at[d],
            recv_sem=rrecv.at[lobs],
            device_id=(d, lgx, gy),
            device_id_type=MESH,
        )

    for d in range(NP):

        @pl.when(jnp.logical_not(jnp.logical_and(stays, obs == d)))
        def _(d=d):
            reduce_copy(d).start()

    for d in range(NP):

        @pl.when(jnp.logical_not(is_me(d)))
        def _(d=d):
            pltpu.make_async_remote_copy(
                src_ref=gpack.at[d],
                dst_ref=gred.at[d],
                send_sem=rsend.at[d],
                recv_sem=rrecv.at[d],
                device_id=partner,
                device_id_type=MESH,
            ).wait_recv()

    for h in range(2):
        total = gred[0, pl.ds(h * 8, 8), :]
        for d in range(1, NP):
            total = total + gred[d, pl.ds(h * 8, 8), :]
        for x in range(NX):
            turned = pltpu.roll(total, NZ - LP * x, 1) if x else total
            grad_ref[x, pl.ds(h * 8, 8), :] = turned[:, :LP]

    for d in range(NP):

        @pl.when(jnp.logical_not(jnp.logical_and(stays, obs == d)))
        def _(d=d):
            reduce_copy(d).wait_send()

    for n in range(NS):
        for target in range(NP):

            @pl.when(jnp.logical_not(is_me(target)))
            def _(n=n, target=target):
                gather_copy(n, target).wait_send()

    @pl.when(moves)
    def _():
        for k in range(2 * NO):
            swap_out(k).wait()

    @pl.when(stays)
    def _():
        for k in range(2 * NO):
            keep_out(k).wait()


def local(*args):
    hbm = pl.BlockSpec(memory_space=pl.ANY)
    vmem = pl.BlockSpec(memory_space=pltpu.VMEM)
    smem = pl.BlockSpec(memory_space=pltpu.SMEM)
    dma = pltpu.SemaphoreType.DMA
    return pl.pallas_call(
        kernel,
        out_shape=(
            jax.ShapeDtypeStruct((2, NO, NX, NY, NZ), F32),
            jax.ShapeDtypeStruct((NX, NY, LP), F32),
        ),
        in_specs=[hbm, hbm, hbm, hbm, hbm, vmem, smem, smem],
        out_specs=(hbm, vmem),
        scratch_shapes=[
            pltpu.VMEM((NS, 4, NX, NY, LP), F32),
            pltpu.VMEM((NS, 64, NZ), F32),
            pltpu.VMEM((NS, NP, 64, NZ), F32),
            pltpu.VMEM((NX, 2 * NO * NY, NZ), F32),
            pltpu.VMEM((ST, 5, 8, NZ), F32),
            pltpu.VMEM((ST, 5, 8, NZ), F32),
            pltpu.VMEM((ST, 2, NX + 2, ROWS, NZ), F32),
            pltpu.VMEM((ST, 2, 2, XG * 8, NZ), F32),
            pltpu.VMEM((ST, 2, 2, XG * 8, NZ), F32),
            pltpu.VMEM((NS, 8, NX, NJ * 8, NZ), F32),
            pltpu.VMEM((8, NX, SO * NY, NZ), F32),
            pltpu.VMEM((NX + 2, SO * NY, NZ), F32),
            pltpu.VMEM((NS, NX * NY, NZ), F32),
            pltpu.VMEM((NS, 2, 8, NZ), F32),
            pltpu.VMEM((NS, 2, NY, NZ), F32),
            pltpu.VMEM((NS, 2, 8, NZ), F32),
            pltpu.VMEM((ST, NX, ROWS, NZ), F32),
            pltpu.VMEM((NX, NJ * 8, NZ), F32),
            pltpu.VMEM((NX, 8 * NJ, NZ), F32),
            pltpu.VMEM((NP, NY, NZ), F32),
            pltpu.VMEM((NP, NY, NZ), F32),
            pltpu.VMEM((NX, 2 * NO * NY, NZ), F32),
            dma((NS, 4)),
            dma((NS, NP)),
            dma((NS, NP)),
            dma((2 * NO,)),
            dma((2 * NO,)),
            dma((2,)),
            dma((ST, 2, 4)),
            dma((ST, 2, 4)),
            dma((NS, 4)),
            dma((NS, 4)),
            dma((2 * NO,)),
            dma((2 * NO,)),
            dma((NP,)),
            dma((NP,)),
        ],
        compiler_params=pltpu.CompilerParams(
            collective_id=0, has_side_effects=True, vmem_limit_bytes=67043328
        ),
    )(*args)


def solution(mesh):
    return jax.shard_map(
        local,
        mesh=mesh,
        in_specs=(
            P(None, "obs", "gx", "gy", None),
            P(None, "gx", "gy", "obs"),
            P(None, "gx", "gy", "obs"),
            P(None, "gx", "gy", "obs"),
            P(None, "gx", "gy", "obs"),
            P(None, "obs", None),
            P("obs"),
            P("obs"),
        ),
        out_specs=(P(None, "obs", "gx", "gy", None), P("gx", "gy", "obs")),
        check_vma=False,
    )
```

```python
import functools

import jax
import jax.numpy as jnp
from jax import lax
from jax.experimental import pallas as pl
from jax.experimental.pallas import tpu as pltpu
from jax.sharding import PartitionSpec as P

MESH = pl.DeviceIdType.MESH
F32 = jnp.float32
ITERS = 4
LAG = 0
UNROLL = 4
NX, NY, NZ = 8, 16, 128
NS = 3
NO = 4
NP = 8
LP = NZ // NP
SO = 2
ST = NO // SO
NQ = 8 // SO
NJ = NY // NQ
NG = NQ // 2
XG = NX // NG
ROWS = 2 * NJ * 8
NE = NJ + 2
ROUNDS = NS * ITERS // 2
AP, BP, AT, BT, RPC, IP, RTC, KK = range(8)


PLAN = {
    "start": (("forward", 2), ("send", 1), ("prepare", 2), ("set_up", 0), ("set_up", 1), ("complete", 2)),
    (0, 0): (("forward", 1),),
    (1, 0): (("prepare", 1),),
    (1, 1): (("complete", 1), ("send", 0)),
    (2, 1): (("forward", 0),),
    (3, 0): (("prepare", 0),),
    (3, 1): (("complete", 0),),
}


def role(obs, gx):
    return 2 * (obs // 2) + gx % 2, 2 * (gx // 2) + obs % 2


def regroup(tiles, lane_group):
    turned = [pltpu.roll(t, LP * d, 1) if d else t for d, t in enumerate(tiles)]
    outs = []
    for x in range(NP):
        mixed = turned[(NP - 1 - x) % NP]
        for g in range(NP - 1):
            mixed = jnp.where(lane_group == g, turned[(g - x) % NP], mixed)
        outs.append(pltpu.roll(mixed, NZ - LP * x, 1) if x else mixed)
    return outs


def kernel(
    cost_ref, pore_ref, heat_ref, dil_ref, cond_ref, resid_ref, pos_ref, wgt_ref,
    out_ref, grad_ref,
    saved, pack, gath, raw, meta, meta_in, state, mid, edge, ysend, yrecv, corner,
    coef, crep, ccol, prep_pore, yfield, ycol, prow, pcol, right, gacc, gsum, gpack, gred, outst,
    load_sem, gsend, grecv, gfwd, ssend, srecv, msem, hsend, hrecv, csend, crecv, psend, precv, osend, orecv, rsend, rrecv,
):
    obs, gx, gy = lax.axis_index("obs"), lax.axis_index("gx"), lax.axis_index("gy")
    lobs, lgx = role(obs, gx)
    stays = jnp.logical_and(lobs == obs, lgx == gx)
    moves = jnp.logical_not(stays)
    zh, yy = obs // 2, gx // 2
    ngx, ngy = lax.axis_size("gx"), lax.axis_size("gy")

    lane = lax.broadcasted_iota(jnp.int32, (8, NZ), 1)
    sub = lax.broadcasted_iota(jnp.int32, (8, NZ), 0)
    lane_group = lane // LP
    first_lane, last_lane = lane == 0, lane == NZ - 1

    exists = (lgx > 0, lgx < ngx - 1, gy > 0, gy < ngy - 1)
    xm = role(lobs, jnp.maximum(lgx - 1, 0))
    xp = role(lobs, jnp.minimum(lgx + 1, ngx - 1))
    near = (
        (xm[0], xm[1], gy),
        (xp[0], xp[1], gy),
        (obs, gx, jnp.maximum(gy - 1, 0)),
        (obs, gx, jnp.minimum(gy + 1, ngy - 1)),
    )
    slant_exists = [jnp.logical_and(exists[cx], exists[2 + cy]) for cx in range(2) for cy in range(2)]
    slant = [(near[cx][0], near[cx][1], near[2 + cy][2]) for cx in range(2) for cy in range(2)]
    partner = (lobs, lgx, gy)

    fields = (pore_ref, heat_ref, dil_ref, cond_ref)

    def load(n, f):
        return pltpu.make_async_copy(fields[f].at[n], saved.at[n, f], load_sem.at[n, f])

    for n in range(NS - 1, -1, -1):
        for f in range(4):
            load(n, f).start()

    zero = jnp.zeros((8, NZ), F32)
    for st in range(ST):
        for par in range(2):
            for row in (0, 1, NX + 2, NX + 3):
                state[st, par, row] = jnp.zeros((ROWS, NZ), F32)
    yrecv[...] = jnp.zeros(yrecv.shape, F32)
    corner[...] = jnp.zeros(corner.shape, F32)
    prow[...] = jnp.zeros(prow.shape, F32)
    pcol[...] = jnp.zeros(pcol.shape, F32)

    barrier = pltpu.get_barrier_semaphore()
    for zz in range(4):
        for core in range(2):
            for low in range(2):
                there = (2 * zz + core, 2 * yy + low, gy)

                @pl.when(jnp.logical_or(there[0] != obs, there[1] != gx))
                def _(there=there):
                    pl.semaphore_signal(barrier, inc=1, device_id=there, device_id_type=MESH)

    for k in range(4):

        @pl.when(exists[k])
        def _(k=k):
            pl.semaphore_signal(barrier, inc=1, device_id=near[k], device_id_type=MESH)

        @pl.when(slant_exists[k])
        def _(k=k):
            pl.semaphore_signal(barrier, inc=1, device_id=slant[k], device_id_type=MESH)

    count = 15
    for k in range(4):
        count = count + exists[k].astype(jnp.int32) + slant_exists[k].astype(jnp.int32)
    pl.semaphore_wait(barrier, count)

    srow = sub // NQ
    squarter = sub % NQ
    for st in range(ST):
        for n in range(NS):
            tile = zero
            for o in range(SO):
                k = st * SO + o
                tile = jnp.where(srow == o, jnp.broadcast_to(resid_ref[n, k : k + 1, :], (8, NZ)), tile)
            meta[st, n] = tile
        pos = jnp.zeros((8, NZ), jnp.int32)
        wgt = jnp.zeros((8, NZ), jnp.int32)
        for o in range(SO):
            pos = jnp.where(srow == o, pos_ref[st * SO + o], pos)
            wgt = jnp.where(srow == o, wgt_ref[st * SO + o], wgt)
        meta[st, 3] = pos.astype(F32)
        meta[st, 4] = wgt.astype(F32)

    def gather_copy(n, zt):
        return pltpu.make_async_remote_copy(
            src_ref=pack.at[n],
            dst_ref=gath.at[n, obs],
            send_sem=gsend.at[n, zt],
            recv_sem=grecv.at[n, obs],
            device_id=(2 * zt + gx % 2, gx, gy),
            device_id_type=MESH,
        )

    zl = gx % 2
    onward = (2 * lax.rem(zh + 3 + 2 * zl, 4) + zl, 2 * yy + 1 - zl, gy)

    def forward_copy(n, d):
        return pltpu.make_async_remote_copy(
            src_ref=gath.at[n, d],
            dst_ref=gath.at[n, d],
            send_sem=gfwd.at[n, d],
            recv_sem=grecv.at[n, d],
            device_id=onward,
            device_id_type=MESH,
        )

    def forward(n):
        @pl.when(stays)
        def _():
            for off in (0, 1, 3, 2):
                for core in range(2):
                    d = 2 * lax.rem(zh + off, 4) + core
                    if off == 0:

                        @pl.when(obs != d)
                        def _(d=d):
                            forward_copy(n, d).wait_recv()

                    else:
                        forward_copy(n, d).wait_recv()
                    forward_copy(n, d).start()

    def is_me(target):
        return jnp.logical_and(stays, lobs == target)

    def send_saved(n):
        for f in range(4):
            load(n, f).wait()
        for f in range(4):
            for h in range(2):
                packed = saved_tile(n, f, 0, h)
                for x in range(1, NX):
                    packed = jnp.where(
                        lane_group == x, pltpu.roll(saved_tile(n, f, x, h), LP * x, 1), packed
                    )
                pack[n, pl.ds((f * 2 + h) * 8, 8), :] = packed

                @pl.when(stays)
                def _(packed=packed, f=f, h=h):
                    gath[n, obs, pl.ds((f * 2 + h) * 8, 8), :] = packed

        for zt in range(4):

            @pl.when(jnp.logical_not(jnp.logical_and(stays, zh == zt)))
            def _(zt=zt):
                gather_copy(n, zt).start()

    def saved_tile(n, f, x, h):
        piece = saved[n, f, x, pl.ds(h * 8, 8), :]
        return jnp.concatenate([piece, jnp.zeros((8, NZ - LP), F32)], axis=1)

    def swap_in(k):
        return pltpu.make_async_remote_copy(
            src_ref=cost_ref.at[k // NO, k % NO],
            dst_ref=raw.at[:, pl.ds(k * NY, NY), :],
            send_sem=ssend.at[k],
            recv_sem=srecv.at[k],
            device_id=partner,
            device_id_type=MESH,
        )

    def keep_in(k):
        return pltpu.make_async_copy(
            cost_ref.at[k // NO, k % NO], raw.at[:, pl.ds(k * NY, NY), :], srecv.at[k]
        )

    def send_meta():
        return pltpu.make_async_remote_copy(
            src_ref=meta, dst_ref=meta_in, send_sem=msem.at[0], recv_sem=msem.at[1], device_id=partner, device_id_type=MESH
        )

    def streams_obs(st):
        return [f * NO + st * SO + o for f in range(2) for o in range(SO)]

    send_saved(NS - 1)

    @pl.when(moves)
    def _():
        send_meta().start()
        for st in range(ST):
            for k in streams_obs(st):
                swap_in(k).start()

    @pl.when(stays)
    def _():
        for st in range(ST):
            for k in streams_obs(st):
                keep_in(k).start()
        meta_in[...] = meta[...]

    def halo(st, par, k):
        if k == 0:
            src, dst = state.at[st, par, pl.ds(2, 2)], state.at[st, par, pl.ds(NX + 2, 2)]
        elif k == 1:
            src, dst = state.at[st, par, pl.ds(NX, 2)], state.at[st, par, pl.ds(0, 2)]
        elif k == 2:
            src, dst = ysend.at[st, par, 0], yrecv.at[st, par, 1]
        else:
            src, dst = ysend.at[st, par, 1], yrecv.at[st, par, 0]
        return pltpu.make_async_remote_copy(
            src_ref=src,
            dst_ref=dst,
            send_sem=hsend.at[st, par, k],
            recv_sem=hrecv.at[st, par, k ^ 1],
            device_id=near[k],
            device_id_type=MESH,
        )

    def corner_copy(st, par, k):
        cx, cy = k // 2, k % 2
        return pltpu.make_async_remote_copy(
            src_ref=ysend.at[st, par, cy, 0, pl.ds((XG - 1) * 8 if cx else 0, 8)],
            dst_ref=corner.at[st, par, 3 - k],
            send_sem=csend.at[st, par, k],
            recv_sem=crecv.at[st, par, 3 - k],
            device_id=slant[k],
            device_id_type=MESH,
        )

    def start_halos(st, par):
        for k in range(4):

            @pl.when(slant_exists[k])
            def _(k=k):
                corner_copy(st, par, k).start()

        for k in range(4):

            @pl.when(exists[k])
            def _(k=k):
                halo(st, par, k).start()

    def wait_sent(st, par):
        for k in range(4):

            @pl.when(exists[k])
            def _(k=k):
                halo(st, par, k).wait_send()

            @pl.when(slant_exists[k])
            def _(k=k):
                corner_copy(st, par, k).wait_send()

    def wait_halos(st, par):
        for k in range(4):

            @pl.when(exists[k])
            def _(k=k):
                halo(st, par, k ^ 1).wait_recv()

            @pl.when(slant_exists[k])
            def _(k=k):
                corner_copy(st, par, 3 - k).wait_recv()

    def y_message(st, par, xg, firsts, lasts):
        for col in range(2):
            low, high = firsts[0][col], pltpu.roll(lasts[0][col], (9 - NQ) % 8, 0)
            for i in range(1, NQ):
                low = jnp.where(squarter == i, pltpu.roll(firsts[i][col], i, 0), low)
                turned = lasts[i][col] if i == NQ - 1 else pltpu.roll(lasts[i][col], (9 + i - NQ) % 8, 0)
                high = jnp.where(squarter == i, turned, high)
            ysend[st, par, 0, col, pl.ds(xg * 8, 8), :] = low
            ysend[st, par, 1, col, pl.ds(xg * 8, 8), :] = high

    def core(f, j):
        return pl.ds((f * NJ + j) * 8, 8)

    def ext(f, j):
        return pl.ds((f * NE + j + 1) * 8, 8)

    def set_up(st):
        @pl.when(moves)
        def _():
            for k in streams_obs(st):
                swap_in(k).wait()

        @pl.when(stays)
        def _():
            for k in streams_obs(st):
                keep_in(k).wait()

        def first_rows(xg, _):
            firsts, lasts = [], []
            for g in range(NG):
                x = xg + g * XG
                for f in range(2):
                    start = (f * NO + st * SO) * NY
                    tiles = [raw[x, pl.ds(start + j, 8, stride=NJ), :] for j in range(NJ)]
                    for j in range(NJ):
                        state[st, 0, x + 2, core(f, j), :] = tiles[j]
                    firsts.append(tiles[:2])
                    lasts.append((tiles[-1], tiles[-2]))
            y_message(st, 0, xg, firsts, lasts)
            return 0

        lax.fori_loop(0, XG, first_rows, 0)
        start_halos(st, 0)

    def around(tiles, up, down):
        sums = []
        for j, (above, below) in enumerate(zip(up, down)):
            here = tiles[j + 1]
            total = above + below + tiles[j] + tiles[j + 2]
            deep = jnp.where(first_lane, 0.0, pltpu.roll(here, 1, 1))
            shallow = jnp.where(last_lane, 0.0, pltpu.roll(here, NZ - 1, 1))
            sums.append(total + deep + shallow)
        return sums

    def before_of(inner, outside):
        return jnp.where(squarter == 0, outside, pltpu.roll(inner, 1, 0))

    def after_of(inner, outside):
        return jnp.where(squarter == NQ - 1, outside, pltpu.roll(inner, 7, 0))

    def slot_low(tile, i):
        return pltpu.roll(tile, 8 - i, 0) if i else tile

    def slot_high(tile, i):
        return pltpu.roll(tile, NQ - 1 - i, 0) if i < NQ - 1 else tile

    def fill_edges(st, par):
        def rows(xg, _):
            lows = [yrecv[st, par, 0, col, pl.ds(xg * 8, 8), :] for col in range(2)]
            highs = [yrecv[st, par, 1, col, pl.ds(xg * 8, 8), :] for col in range(2)]
            for g in range(NG):
                x = xg + g * XG
                for f in range(2):
                    i = 2 * g + f
                    for col in range(2):
                        inner = state[st, par, x + 2, core(f, NJ - 1 - col), :]
                        edge[st, x + 1, f, 1 - col] = before_of(inner, slot_low(lows[col], i))
                        inner = state[st, par, x + 2, core(f, col), :]
                        edge[st, x + 1, f, 2 + col] = after_of(inner, slot_high(highs[col], i))
            return 0

        lax.fori_loop(0, XG, rows, 0, unroll=2)
        for cx, x, g in ((0, -1, NG - 1), (1, NX, 0)):
            for f in range(2):
                i = 2 * g + f
                inner = state[st, par, x + 2, core(f, NJ - 1), :]
                edge[st, x + 1, f, 1] = before_of(inner, slot_low(corner[st, par, 2 * cx], i))
                inner = state[st, par, x + 2, core(f, 0), :]
                edge[st, x + 1, f, 2] = after_of(inner, slot_high(corner[st, par, 2 * cx + 1], i))

    def wide(st, par, x, f, reach):
        tiles = [state[st, par, x + 2, core(f, j), :] for j in range(NJ)]
        low = [edge[st, x + 1, f, e] for e in range(2 - reach, 2)]
        high = [edge[st, x + 1, f, e] for e in range(2, 2 + reach)]
        return low + tiles + high

    def relaxed(st, n, x, j, near_p, near_t, old_t):
        at, at_t = ext(0, j), ext(1, j)
        new_p = right[st, x + 1, at, :] + coef[n, AP, x + 1, at, :] * near_p + coef[n, BP, x + 1, at, :] * old_t
        new_t = right[st, x + 1, at_t, :] + coef[n, AT, x + 1, at, :] * near_t + coef[n, BT, x + 1, at, :] * new_p
        return new_p, new_t

    def first_sweep(st, par, n):
        def row(x, reach):
            here, sums = [], []
            for f in range(2):
                tiles = wide(st, par, x, f, reach + 1)
                up, down = wide(st, par, x - 1, f, reach), wide(st, par, x + 1, f, reach)
                here.append(tiles)
                sums.append(around(tiles, up, down))
            for p in range(NJ + 2 * reach):
                j = p - reach
                new_p, new_t = relaxed(st, n, x, j, sums[0][p], sums[1][p], here[1][p + 1])
                mid[st, x + 1, ext(0, j), :] = new_p
                mid[st, x + 1, ext(1, j), :] = new_t

        def inner(x, _):
            row(x, 1)
            return 0

        lax.fori_loop(0, NX, inner, 0, unroll=UNROLL)
        row(-1, 0)
        row(NX, 0)

    def second_sweep(st, par, n, last):
        def rows(xg, _):
            firsts, lasts = [], []
            for g in range(NG):
                x = xg + g * XG
                here, sums = [], []
                for f in range(2):
                    tiles = [mid[st, x + 1, ext(f, j), :] for j in range(-1, NJ + 1)]
                    up = [mid[st, x, ext(f, j), :] for j in range(NJ)]
                    down = [mid[st, x + 2, ext(f, j), :] for j in range(NJ)]
                    here.append(tiles)
                    sums.append(around(tiles, up, down))
                new = [[], []]
                for j in range(NJ):
                    new_p, new_t = relaxed(st, n, x, j, sums[0][j], sums[1][j], here[1][j + 1])
                    state[st, 1 - par, x + 2, core(0, j), :] = new_p
                    state[st, 1 - par, x + 2, core(1, j), :] = new_t
                    new[0].append(new_p)
                    new[1].append(new_t)
                for f in range(2):
                    firsts.append(new[f][:2])
                    lasts.append((new[f][-1], new[f][-2]))
            if not last:
                y_message(st, 1 - par, xg, firsts, lasts)
            return 0

        lax.fori_loop(0, XG, rows, 0, unroll=UNROLL // 2)

    base_cell = (lgx * NX) * (ngy * NY) + gy * NY

    def field_halo(n, k):
        if k == 0:
            src, dst = yfield.at[n, :, pl.ds(0, NY)], prow.at[n, 1]
        elif k == 1:
            src, dst = yfield.at[n, :, pl.ds((NX - 1) * NY, NY)], prow.at[n, 0]
        elif k == 2:
            src, dst = ycol.at[n, 0], pcol.at[n, 1]
        else:
            src, dst = ycol.at[n, 1], pcol.at[n, 0]
        return pltpu.make_async_remote_copy(
            src_ref=src,
            dst_ref=dst,
            send_sem=psend.at[n, k],
            recv_sem=precv.at[n, k ^ 1],
            device_id=near[k],
            device_id_type=MESH,
        )

    def repeat(ref, lead, h, value):
        for o in range(SO):
            ref[(*lead, pl.ds(o * NY + h * 8, 8), slice(None))] = value

    def factors(pore, heat, dil, perm):
        store_p = jnp.exp(dil)
        store_t = jnp.exp(0.5 * heat)
        coupling = 0.2 * jnp.tanh(pore)
        inv_p = 1.0 / (store_p + 6.0 * perm)
        inv_t = 1.0 / (store_t + 12.0)
        return (
            perm * inv_p, coupling * inv_p, 2.0 * inv_t, coupling * inv_t,
            store_p * inv_p, inv_p, store_t * inv_t,
        )

    def prepare(n):
        @pl.when(moves)
        def _():
            for d in range(NP):
                forward_copy(n, d).wait_recv()

        for h in range(2):
            whole = [
                regroup([gath[n, d, pl.ds((f * 2 + h) * 8, 8), :] for d in range(NP)], lane_group) for f in range(4)
            ]
            for f in range(4):
                for x in range(NX):
                    yfield[n, f, pl.ds(x * NY + h * 8, 8), :] = whole[f][x]
        for f in range(4):
            for side, y in ((0, 0), (1, NY - 1)):
                ycol[n, side, f] = yfield[n, f, pl.ds(y, NX, stride=NY), :]
        for k in range(4):

            @pl.when(exists[k])
            def _(k=k):
                field_halo(n, k).start()

        def row(x, _):
            for h in range(2):
                values = [yfield[n, f, pl.ds(pl.multiple_of(x * NY + h * 8, 8), 8), :] for f in range(4)]
                for c, value in enumerate(factors(*values)):
                    repeat(crep, (c, x + 1), h, value)
                repeat(crep, (KK, x + 1), h, values[3])
                repeat(prep_pore, (x + 1,), h, values[0])
            return 0

        lax.fori_loop(0, NX, row, 0, unroll=2)

    def complete(n):
        for k in range(4):

            @pl.when(exists[k])
            def _(k=k):
                field_halo(n, k ^ 1).wait_recv()
                field_halo(n, k).wait_send()

        for side, x in ((0, -1), (1, NX)):
            for h in range(2):
                values = [prow[n, side, f, pl.ds(h * 8, 8), :] for f in range(4)]
                for c, value in enumerate(factors(*values)):
                    repeat(crep, (c, x + 1), h, jnp.where(exists[side], value, 0.0))
                repeat(prep_pore, (x + 1,), h, values[0])
            values = [pcol[n, side, f] for f in range(4)]
            for c, value in enumerate(factors(*values)):
                ccol[c, side] = jnp.where(exists[2 + side], value, 0.0)

        def tiles_of(c, x):
            tiles = [crep[c, x + 1, pl.ds(j, 8, stride=NJ), :] for j in range(NJ)]
            for j in range(NJ):
                coef[n, c, x + 1, ext(0, j), :] = tiles[j]
            return tiles

        def spread(x, _):
            for c in range(7):
                tiles = tiles_of(c, x)
                low, high = (jnp.broadcast_to(ccol[c, side, pl.ds(x, 1), :], (8, NZ)) for side in range(2))
                coef[n, c, x + 1, ext(0, -1), :] = before_of(tiles[-1], low)
                coef[n, c, x + 1, ext(0, NJ), :] = after_of(tiles[0], high)
            tiles, up, down = (
                [prep_pore[x + dx, pl.ds(j, 8, stride=NJ), :] for j in range(NJ)] for dx in (1, 0, 2)
            )
            low, high = (jnp.broadcast_to(pcol[n, side, 0, pl.ds(x, 1), :], (8, NZ)) for side in range(2))
            ring = [before_of(tiles[-1], low), *tiles, after_of(tiles[0], high)]
            sums = around(ring, up, down)
            for j in range(NJ):
                perm = crep[KK, x + 1, pl.ds(j, 8, stride=NJ), :]
                coef[n, KK, x + 1, ext(0, j), :] = perm * (sums[j] - 6.0 * tiles[j])
            return 0

        lax.fori_loop(0, NX, spread, 0, unroll=2)
        for c in range(7):
            tiles_of(c, -1)
            tiles_of(c, NX)

    def right_sides(st, par, n):
        source = meta_in[st, n]
        cell = meta_in[st, 3] - (NJ * squarter + base_cell).astype(F32)

        def row(x, reach):
            tiles = [wide(st, par, x, f, reach) for f in range(2)]
            for p in range(NJ + 2 * reach):
                j = p - reach
                at = ext(0, j)
                mine = cell == jnp.asarray(x * (ngy * NY) + j).astype(F32)
                term = jnp.where(mine, source, 0.0)
                right[st, x + 1, at, :] = coef[n, RPC, x + 1, at, :] * tiles[0][p] + coef[n, IP, x + 1, at, :] * term
                right[st, x + 1, ext(1, j), :] = coef[n, RTC, x + 1, at, :] * tiles[1][p]

        def inner(x, _):
            row(x, 1)
            return 0

        lax.fori_loop(0, NX, inner, 0, unroll=2)
        row(-1, 0)
        row(NX, 0)

    def add_gradient(st, par, n):
        weight = meta_in[st, 4]

        def row(x, _):
            for j in range(NJ):
                at = pl.ds(j * 8, 8)
                gacc[x, at, :] += coef[n, KK, x + 1, ext(0, j), :] * (weight * state[st, par, x + 2, core(0, j), :])
            return 0

        lax.fori_loop(0, NX, row, 0, unroll=2)

    def swap_out(k):
        return pltpu.make_async_remote_copy(
            src_ref=outst.at[:, pl.ds(k * NY, NY), :],
            dst_ref=out_ref.at[k // NO, k % NO],
            send_sem=osend.at[k],
            recv_sem=orecv.at[k],
            device_id=partner,
            device_id_type=MESH,
        )

    def keep_out(k):
        return pltpu.make_async_copy(
            outst.at[:, pl.ds(k * NY, NY), :], out_ref.at[k // NO, k % NO], orecv.at[k]
        )

    def finish(st):
        def row(x, _):
            for f in range(2):
                for j in range(NJ):
                    outst[x, pl.ds((f * NO + st * SO) * NY + j, 8, stride=NJ), :] = state[
                        st, ROUNDS % 2, x + 2, core(f, j), :
                    ]
            return 0

        lax.fori_loop(0, NX, row, 0)

        @pl.when(moves)
        def _():
            for k in streams_obs(st):
                swap_out(k).start()

        @pl.when(stays)
        def _():
            for k in streams_obs(st):
                keep_out(k).start()

    def round_of(st, r):
        n, par = NS - 1 - r // 2, r % 2
        wait_halos(st, par)
        if r > 0:
            wait_sent(st, 1 - par)
        fill_edges(st, par)
        if r % 2 == 0:
            right_sides(st, par, n)
        first_sweep(st, par, n)
        second_sweep(st, par, n, r == ROUNDS - 1)
        if r < ROUNDS - 1:
            start_halos(st, 1 - par)
        else:
            finish(st)
        if r % 2 == 1:
            add_gradient(st, 1 - par, n)

    gacc[...] = jnp.zeros(gacc.shape, F32)
    plan = PLAN
    todo = {
        "send": send_saved, "forward": forward, "prepare": prepare, "complete": complete, "set_up": set_up,
    }

    def do(when):
        for what, n in plan.get(when, ()):
            todo[what](n)

    do("start")

    @pl.when(moves)
    def _():
        send_meta().wait()

    for r in range(ROUNDS + LAG * (ST - 1)):
        for st in range(ST):
            if 0 <= r - LAG * st < ROUNDS:
                round_of(st, r - LAG * st)
            do((r, st))
    for st in range(ST):
        wait_sent(st, (ROUNDS - 1) % 2)

    for x in range(NX):
        for j in range(NJ):
            total = gacc[x, pl.ds(j * 8, 8), :]
            for o in range(1, SO):
                total = total + pltpu.roll(gacc[x, pl.ds(j * 8, 8), :], NQ * o, 0)
            gsum[x, pl.ds(j, 8, stride=NJ), :] = total
    for h in range(2):
        whole = [gsum[x, pl.ds(h * 8, 8), :] for x in range(NX)]
        for d, tile in enumerate(regroup(whole, lane_group)):
            gpack[d, pl.ds(h * 8, 8), :] = tile

            @pl.when(jnp.logical_and(stays, obs == d))
            def _(tile=tile, h=h):
                gred[lobs, pl.ds(h * 8, 8), :] = tile

    def reduce_copy(d):
        return pltpu.make_async_remote_copy(
            src_ref=gpack.at[d],
            dst_ref=gred.at[lobs],
            send_sem=rsend.at[d],
            recv_sem=rrecv.at[lobs],
            device_id=(d, lgx, gy),
            device_id_type=MESH,
        )

    for d in range(NP):

        @pl.when(jnp.logical_not(jnp.logical_and(stays, obs == d)))
        def _(d=d):
            reduce_copy(d).start()

    for d in range(NP):

        @pl.when(jnp.logical_not(is_me(d)))
        def _(d=d):
            pltpu.make_async_remote_copy(
                src_ref=gpack.at[d],
                dst_ref=gred.at[d],
                send_sem=rsend.at[d],
                recv_sem=rrecv.at[d],
                device_id=partner,
                device_id_type=MESH,
            ).wait_recv()

    for h in range(2):
        total = gred[0, pl.ds(h * 8, 8), :]
        for d in range(1, NP):
            total = total + gred[d, pl.ds(h * 8, 8), :]
        for x in range(NX):
            turned = pltpu.roll(total, NZ - LP * x, 1) if x else total
            grad_ref[x, pl.ds(h * 8, 8), :] = turned

    for d in range(NP):

        @pl.when(jnp.logical_not(jnp.logical_and(stays, obs == d)))
        def _(d=d):
            reduce_copy(d).wait_send()

    for n in range(NS):
        for zt in range(4):

            @pl.when(jnp.logical_not(jnp.logical_and(stays, zh == zt)))
            def _(n=n, zt=zt):
                gather_copy(n, zt).wait_send()

        @pl.when(stays)
        def _(n=n):
            for d in range(NP):
                forward_copy(n, d).wait_send()

    @pl.when(moves)
    def _():
        for k in range(2 * NO):
            swap_out(k).wait()

    @pl.when(stays)
    def _():
        for k in range(2 * NO):
            keep_out(k).wait()


def local(*args):
    hbm = pl.BlockSpec(memory_space=pl.ANY)
    vmem = pl.BlockSpec(memory_space=pltpu.VMEM)
    smem = pl.BlockSpec(memory_space=pltpu.SMEM)
    dma = pltpu.SemaphoreType.DMA
    costates, gradient = pl.pallas_call(
        kernel,
        out_shape=(
            jax.ShapeDtypeStruct((2, NO, NX, NY, NZ), F32),
            jax.ShapeDtypeStruct((NX, NY, NZ), F32),
        ),
        in_specs=[hbm, hbm, hbm, hbm, hbm, vmem, smem, smem],
        out_specs=(hbm, vmem),
        scratch_shapes=[
            pltpu.VMEM((NS, 4, NX, NY, LP), F32),
            pltpu.VMEM((NS, 64, NZ), F32),
            pltpu.VMEM((NS, NP, 64, NZ), F32),
            pltpu.VMEM((NX, 2 * NO * NY, NZ), F32),
            pltpu.VMEM((ST, 5, 8, NZ), F32),
            pltpu.VMEM((ST, 5, 8, NZ), F32),
            pltpu.VMEM((ST, 2, NX + 4, ROWS, NZ), F32),
            pltpu.VMEM((ST, NX + 2, 2 * NE * 8, NZ), F32),
            pltpu.VMEM((ST, NX + 2, 2, 4, 8, NZ), F32),
            pltpu.VMEM((ST, 2, 2, 2, XG * 8, NZ), F32),
            pltpu.VMEM((ST, 2, 2, 2, XG * 8, NZ), F32),
            pltpu.VMEM((ST, 2, 4, 8, NZ), F32),
            pltpu.VMEM((NS, 8, NX + 2, NE * 8, NZ), F32),
            pltpu.VMEM((8, NX + 2, SO * NY, NZ), F32),
            pltpu.VMEM((7, 2, 8, NZ), F32),
            pltpu.VMEM((NX + 2, SO * NY, NZ), F32),
            pltpu.VMEM((NS, 4, NX * NY, NZ), F32),
            pltpu.VMEM((NS, 2, 4, 8, NZ), F32),
            pltpu.VMEM((NS, 2, 4, NY, NZ), F32),
            pltpu.VMEM((NS, 2, 4, 8, NZ), F32),
            pltpu.VMEM((ST, NX + 2, 2 * NE * 8, NZ), F32),
            pltpu.VMEM((NX, NJ * 8, NZ), F32),
            pltpu.VMEM((NX, 8 * NJ, NZ), F32),
            pltpu.VMEM((NP, NY, NZ), F32),
            pltpu.VMEM((NP, NY, NZ), F32),
            pltpu.VMEM((NX, 2 * NO * NY, NZ), F32),
            dma((NS, 4)),
            dma((NS, 4)),
            dma((NS, NP)),
            dma((NS, NP)),
            dma((2 * NO,)),
            dma((2 * NO,)),
            dma((2,)),
            dma((ST, 2, 4)),
            dma((ST, 2, 4)),
            dma((ST, 2, 4)),
            dma((ST, 2, 4)),
            dma((NS, 4)),
            dma((NS, 4)),
            dma((2 * NO,)),
            dma((2 * NO,)),
            dma((NP,)),
            dma((NP,)),
        ],
        compiler_params=pltpu.CompilerParams(
            collective_id=0, has_side_effects=True, vmem_limit_bytes=67043328
        ),
    )(*args)
    return costates, gradient[:, :, :LP]


def solution(mesh):
    return jax.shard_map(
        local,
        mesh=mesh,
        in_specs=(
            P(None, "obs", "gx", "gy", None),
            P(None, "gx", "gy", "obs"),
            P(None, "gx", "gy", "obs"),
            P(None, "gx", "gy", "obs"),
            P(None, "gx", "gy", "obs"),
            P(None, "obs", None),
            P("obs"),
            P("obs"),
        ),
        out_specs=(P(None, "obs", "gx", "gy", None), P("gx", "gy", "obs")),
        check_vma=False,
    )
```

```python
import functools

import jax
import jax.numpy as jnp
from jax import lax
from jax.experimental import pallas as pl
from jax.experimental.pallas import tpu as pltpu
from jax.sharding import PartitionSpec as P

MESH = pl.DeviceIdType.MESH
F32 = jnp.float32
ITERS = 4
LAG = 0
UNROLL = 8
NX, NY, NZ = 8, 16, 128
NS = 3
NO = 4
NP = 8
LP = NZ // NP
SO = 2
ST = NO // SO
NQ = 8 // SO
NJ = NY // NQ
NG = NQ // 2
XG = NX // NG
ROWS = 2 * NJ * 8
NE = NJ + 2
ROUNDS = NS * ITERS // 2
AP, BP, AT, BT, RPC, IP, RTC, KK = range(8)


PLAN = {
    "start": (("forward", 2), ("send", 1), ("prepare", 2), ("set_up", 0), ("set_up", 1), ("complete", 2)),
    (0, 0): (("forward", 1), ("send", 0)),
    (0, 1): (("prepare", 1),),
    (1, 0): (("forward", 0),),
    (1, 1): (("complete", 1),),
    (2, 1): (("prepare", 0),),
    (3, 1): (("complete", 0),),
}


def role(obs, gx):
    return 2 * (obs // 2) + gx % 2, 2 * (gx // 2) + obs % 2


def regroup(tiles, lane_group):
    turned = [pltpu.roll(t, LP * d, 1) if d else t for d, t in enumerate(tiles)]
    outs = []
    for x in range(NP):
        mixed = turned[(NP - 1 - x) % NP]
        for g in range(NP - 1):
            mixed = jnp.where(lane_group == g, turned[(g - x) % NP], mixed)
        outs.append(pltpu.roll(mixed, NZ - LP * x, 1) if x else mixed)
    return outs


def kernel(
    cost_ref, pore_ref, heat_ref, dil_ref, cond_ref, resid_ref, pos_ref, wgt_ref,
    out_ref, grad_ref,
    saved, pack, gath, raw, meta, meta_in, state, mid, edge, ysend, yrecv, corner,
    coef, crep, ccol, prep_pore, yfield, ycol, prow, pcol, right, gacc, gsum, gpack, gred, outst,
    load_sem, gsend, grecv, gfwd, ssend, srecv, msem, hsend, hrecv, csend, crecv, psend, precv, osend, orecv, rsend, rrecv,
):
    obs, gx, gy = lax.axis_index("obs"), lax.axis_index("gx"), lax.axis_index("gy")
    lobs, lgx = role(obs, gx)
    stays = jnp.logical_and(lobs == obs, lgx == gx)
    moves = jnp.logical_not(stays)
    zh, yy = obs // 2, gx // 2
    ngx, ngy = lax.axis_size("gx"), lax.axis_size("gy")

    lane = lax.broadcasted_iota(jnp.int32, (8, NZ), 1)
    sub = lax.broadcasted_iota(jnp.int32, (8, NZ), 0)
    lane_group = lane // LP
    first_lane, last_lane = lane == 0, lane == NZ - 1

    exists = (lgx > 0, lgx < ngx - 1, gy > 0, gy < ngy - 1)
    xm = role(lobs, jnp.maximum(lgx - 1, 0))
    xp = role(lobs, jnp.minimum(lgx + 1, ngx - 1))
    near = (
        (xm[0], xm[1], gy),
        (xp[0], xp[1], gy),
        (obs, gx, jnp.maximum(gy - 1, 0)),
        (obs, gx, jnp.minimum(gy + 1, ngy - 1)),
    )
    slant_exists = [jnp.logical_and(exists[cx], exists[2 + cy]) for cx in range(2) for cy in range(2)]
    slant = [(near[cx][0], near[cx][1], near[2 + cy][2]) for cx in range(2) for cy in range(2)]
    partner = (lobs, lgx, gy)

    fields = (pore_ref, heat_ref, dil_ref, cond_ref)

    def load(n, f):
        return pltpu.make_async_copy(fields[f].at[n], saved.at[n, f], load_sem.at[n, f])

    for n in range(NS - 1, -1, -1):
        for f in range(4):
            load(n, f).start()

    zero = jnp.zeros((8, NZ), F32)
    for st in range(ST):
        for par in range(2):
            for row in (0, 1, NX + 2, NX + 3):
                state[st, par, row] = jnp.zeros((ROWS, NZ), F32)
    yrecv[...] = jnp.zeros(yrecv.shape, F32)
    corner[...] = jnp.zeros(corner.shape, F32)
    prow[...] = jnp.zeros(prow.shape, F32)
    pcol[...] = jnp.zeros(pcol.shape, F32)

    barrier = pltpu.get_barrier_semaphore()
    for zz in range(4):
        for core in range(2):
            for low in range(2):
                there = (2 * zz + core, 2 * yy + low, gy)

                @pl.when(jnp.logical_or(there[0] != obs, there[1] != gx))
                def _(there=there):
                    pl.semaphore_signal(barrier, inc=1, device_id=there, device_id_type=MESH)

    for k in range(4):

        @pl.when(exists[k])
        def _(k=k):
            pl.semaphore_signal(barrier, inc=1, device_id=near[k], device_id_type=MESH)

        @pl.when(slant_exists[k])
        def _(k=k):
            pl.semaphore_signal(barrier, inc=1, device_id=slant[k], device_id_type=MESH)

    count = 15
    for k in range(4):
        count = count + exists[k].astype(jnp.int32) + slant_exists[k].astype(jnp.int32)
    pl.semaphore_wait(barrier, count)

    srow = sub // NQ
    squarter = sub % NQ
    for st in range(ST):
        for n in range(NS):
            tile = zero
            for o in range(SO):
                k = st * SO + o
                tile = jnp.where(srow == o, jnp.broadcast_to(resid_ref[n, k : k + 1, :], (8, NZ)), tile)
            meta[st, n] = tile
        pos = jnp.zeros((8, NZ), jnp.int32)
        wgt = jnp.zeros((8, NZ), jnp.int32)
        for o in range(SO):
            pos = jnp.where(srow == o, pos_ref[st * SO + o], pos)
            wgt = jnp.where(srow == o, wgt_ref[st * SO + o], wgt)
        meta[st, 3] = pos.astype(F32)
        meta[st, 4] = wgt.astype(F32)

    def gather_copy(n, zt):
        return pltpu.make_async_remote_copy(
            src_ref=pack.at[n],
            dst_ref=gath.at[n, obs],
            send_sem=gsend.at[n, zt],
            recv_sem=grecv.at[n, obs],
            device_id=(2 * zt + gx % 2, gx, gy),
            device_id_type=MESH,
        )

    zl = gx % 2
    onward = (2 * lax.rem(zh + 3 + 2 * zl, 4) + zl, 2 * yy + 1 - zl, gy)

    def forward_copy(n, d):
        return pltpu.make_async_remote_copy(
            src_ref=gath.at[n, d],
            dst_ref=gath.at[n, d],
            send_sem=gfwd.at[n, d],
            recv_sem=grecv.at[n, d],
            device_id=onward,
            device_id_type=MESH,
        )

    def forward(n):
        @pl.when(stays)
        def _():
            for off in (0, 1, 3, 2):
                for core in range(2):
                    d = 2 * lax.rem(zh + off, 4) + core
                    if off == 0:

                        @pl.when(obs != d)
                        def _(d=d):
                            forward_copy(n, d).wait_recv()

                    else:
                        forward_copy(n, d).wait_recv()
                    forward_copy(n, d).start()

    def is_me(target):
        return jnp.logical_and(stays, lobs == target)

    def send_saved(n):
        for f in range(4):
            load(n, f).wait()
        for f in range(4):
            for h in range(2):
                packed = saved_tile(n, f, 0, h)
                for x in range(1, NX):
                    packed = jnp.where(
                        lane_group == x, pltpu.roll(saved_tile(n, f, x, h), LP * x, 1), packed
                    )
                pack[n, pl.ds((f * 2 + h) * 8, 8), :] = packed

                @pl.when(stays)
                def _(packed=packed, f=f, h=h):
                    gath[n, obs, pl.ds((f * 2 + h) * 8, 8), :] = packed

        for zt in range(4):

            @pl.when(jnp.logical_not(jnp.logical_and(stays, zh == zt)))
            def _(zt=zt):
                gather_copy(n, zt).start()

    def saved_tile(n, f, x, h):
        piece = saved[n, f, x, pl.ds(h * 8, 8), :]
        return jnp.concatenate([piece, jnp.zeros((8, NZ - LP), F32)], axis=1)

    def swap_in(k):
        return pltpu.make_async_remote_copy(
            src_ref=cost_ref.at[k // NO, k % NO],
            dst_ref=raw.at[:, pl.ds(k * NY, NY), :],
            send_sem=ssend.at[k],
            recv_sem=srecv.at[k],
            device_id=partner,
            device_id_type=MESH,
        )

    def keep_in(k):
        return pltpu.make_async_copy(
            cost_ref.at[k // NO, k % NO], raw.at[:, pl.ds(k * NY, NY), :], srecv.at[k]
        )

    def send_meta():
        return pltpu.make_async_remote_copy(
            src_ref=meta, dst_ref=meta_in, send_sem=msem.at[0], recv_sem=msem.at[1], device_id=partner, device_id_type=MESH
        )

    def streams_obs(st):
        return [f * NO + st * SO + o for f in range(2) for o in range(SO)]

    send_saved(NS - 1)

    @pl.when(moves)
    def _():
        send_meta().start()
        for st in range(ST):
            for k in streams_obs(st):
                swap_in(k).start()

    @pl.when(stays)
    def _():
        for st in range(ST):
            for k in streams_obs(st):
                keep_in(k).start()
        meta_in[...] = meta[...]

    def halo(st, par, k):
        if k == 0:
            src, dst = state.at[st, par, pl.ds(2, 2)], state.at[st, par, pl.ds(NX + 2, 2)]
        elif k == 1:
            src, dst = state.at[st, par, pl.ds(NX, 2)], state.at[st, par, pl.ds(0, 2)]
        elif k == 2:
            src, dst = ysend.at[st, par, 0], yrecv.at[st, par, 1]
        else:
            src, dst = ysend.at[st, par, 1], yrecv.at[st, par, 0]
        return pltpu.make_async_remote_copy(
            src_ref=src,
            dst_ref=dst,
            send_sem=hsend.at[st, par, k],
            recv_sem=hrecv.at[st, par, k ^ 1],
            device_id=near[k],
            device_id_type=MESH,
        )

    def corner_copy(st, par, k):
        cx, cy = k // 2, k % 2
        return pltpu.make_async_remote_copy(
            src_ref=ysend.at[st, par, cy, 0, pl.ds((XG - 1) * 8 if cx else 0, 8)],
            dst_ref=corner.at[st, par, 3 - k],
            send_sem=csend.at[st, par, k],
            recv_sem=crecv.at[st, par, 3 - k],
            device_id=slant[k],
            device_id_type=MESH,
        )

    def start_halos(st, par):
        for k in range(4):

            @pl.when(slant_exists[k])
            def _(k=k):
                corner_copy(st, par, k).start()

        for k in range(4):

            @pl.when(exists[k])
            def _(k=k):
                halo(st, par, k).start()

    def wait_sent(st, par):
        for k in range(4):

            @pl.when(exists[k])
            def _(k=k):
                halo(st, par, k).wait_send()

            @pl.when(slant_exists[k])
            def _(k=k):
                corner_copy(st, par, k).wait_send()

    def wait_halos(st, par):
        for k in range(4):

            @pl.when(exists[k])
            def _(k=k):
                halo(st, par, k ^ 1).wait_recv()

            @pl.when(slant_exists[k])
            def _(k=k):
                corner_copy(st, par, 3 - k).wait_recv()

    def y_message(st, par, xg, firsts, lasts):
        for col in range(2):
            low, high = firsts[0][col], pltpu.roll(lasts[0][col], (9 - NQ) % 8, 0)
            for i in range(1, NQ):
                low = jnp.where(squarter == i, pltpu.roll(firsts[i][col], i, 0), low)
                turned = lasts[i][col] if i == NQ - 1 else pltpu.roll(lasts[i][col], (9 + i - NQ) % 8, 0)
                high = jnp.where(squarter == i, turned, high)
            ysend[st, par, 0, col, pl.ds(xg * 8, 8), :] = low
            ysend[st, par, 1, col, pl.ds(xg * 8, 8), :] = high

    def core(f, j):
        return pl.ds((f * NJ + j) * 8, 8)

    def ext(f, j):
        return pl.ds((f * NE + j + 1) * 8, 8)

    def set_up(st):
        @pl.when(moves)
        def _():
            for k in streams_obs(st):
                swap_in(k).wait()

        @pl.when(stays)
        def _():
            for k in streams_obs(st):
                keep_in(k).wait()

        def first_rows(xg, _):
            firsts, lasts = [], []
            for g in range(NG):
                x = xg + g * XG
                for f in range(2):
                    start = (f * NO + st * SO) * NY
                    tiles = [raw[x, pl.ds(start + j, 8, stride=NJ), :] for j in range(NJ)]
                    for j in range(NJ):
                        state[st, 0, x + 2, core(f, j), :] = tiles[j]
                    firsts.append(tiles[:2])
                    lasts.append((tiles[-1], tiles[-2]))
            y_message(st, 0, xg, firsts, lasts)
            return 0

        lax.fori_loop(0, XG, first_rows, 0)
        start_halos(st, 0)

    def around(tiles, up, down):
        sums = []
        for j, (above, below) in enumerate(zip(up, down)):
            here = tiles[j + 1]
            total = above + below + tiles[j] + tiles[j + 2]
            deep = jnp.where(first_lane, 0.0, pltpu.roll(here, 1, 1))
            shallow = jnp.where(last_lane, 0.0, pltpu.roll(here, NZ - 1, 1))
            sums.append(total + deep + shallow)
        return sums

    def before_of(inner, outside):
        return jnp.where(squarter == 0, outside, pltpu.roll(inner, 1, 0))

    def after_of(inner, outside):
        return jnp.where(squarter == NQ - 1, outside, pltpu.roll(inner, 7, 0))

    def slot_low(tile, i):
        return pltpu.roll(tile, 8 - i, 0) if i else tile

    def slot_high(tile, i):
        return pltpu.roll(tile, NQ - 1 - i, 0) if i < NQ - 1 else tile

    def fill_edges(st, par):
        def rows(xg, _):
            lows = [yrecv[st, par, 0, col, pl.ds(xg * 8, 8), :] for col in range(2)]
            highs = [yrecv[st, par, 1, col, pl.ds(xg * 8, 8), :] for col in range(2)]
            for g in range(NG):
                x = xg + g * XG
                for f in range(2):
                    i = 2 * g + f
                    for col in range(2):
                        inner = state[st, par, x + 2, core(f, NJ - 1 - col), :]
                        edge[st, x + 1, f, 1 - col] = before_of(inner, slot_low(lows[col], i))
                        inner = state[st, par, x + 2, core(f, col), :]
                        edge[st, x + 1, f, 2 + col] = after_of(inner, slot_high(highs[col], i))
            return 0

        lax.fori_loop(0, XG, rows, 0, unroll=2)
        for cx, x, g in ((0, -1, NG - 1), (1, NX, 0)):
            for f in range(2):
                i = 2 * g + f
                inner = state[st, par, x + 2, core(f, NJ - 1), :]
                edge[st, x + 1, f, 1] = before_of(inner, slot_low(corner[st, par, 2 * cx], i))
                inner = state[st, par, x + 2, core(f, 0), :]
                edge[st, x + 1, f, 2] = after_of(inner, slot_high(corner[st, par, 2 * cx + 1], i))

    def wide(st, par, x, f, reach):
        tiles = [state[st, par, x + 2, core(f, j), :] for j in range(NJ)]
        low = [edge[st, x + 1, f, e] for e in range(2 - reach, 2)]
        high = [edge[st, x + 1, f, e] for e in range(2, 2 + reach)]
        return low + tiles + high

    def relaxed(st, n, x, j, near_p, near_t, old_t):
        at, at_t = ext(0, j), ext(1, j)
        new_p = right[st, x + 1, at, :] + coef[n, AP, x + 1, at, :] * near_p + coef[n, BP, x + 1, at, :] * old_t
        new_t = right[st, x + 1, at_t, :] + coef[n, AT, x + 1, at, :] * near_t + coef[n, BT, x + 1, at, :] * new_p
        return new_p, new_t

    def first_sweep(st, par, n):
        def row(x, reach):
            here, sums = [], []
            for f in range(2):
                tiles = wide(st, par, x, f, reach + 1)
                up, down = wide(st, par, x - 1, f, reach), wide(st, par, x + 1, f, reach)
                here.append(tiles)
                sums.append(around(tiles, up, down))
            for p in range(NJ + 2 * reach):
                j = p - reach
                new_p, new_t = relaxed(st, n, x, j, sums[0][p], sums[1][p], here[1][p + 1])
                mid[st, x + 1, ext(0, j), :] = new_p
                mid[st, x + 1, ext(1, j), :] = new_t

        def inner(x, _):
            row(x, 1)
            return 0

        lax.fori_loop(0, NX, inner, 0, unroll=UNROLL)
        row(-1, 0)
        row(NX, 0)

    def second_sweep(st, par, n, last):
        def rows(xg, _):
            firsts, lasts = [], []
            for g in range(NG):
                x = xg + g * XG
                here, sums = [], []
                for f in range(2):
                    tiles = [mid[st, x + 1, ext(f, j), :] for j in range(-1, NJ + 1)]
                    up = [mid[st, x, ext(f, j), :] for j in range(NJ)]
                    down = [mid[st, x + 2, ext(f, j), :] for j in range(NJ)]
                    here.append(tiles)
                    sums.append(around(tiles, up, down))
                new = [[], []]
                for j in range(NJ):
                    new_p, new_t = relaxed(st, n, x, j, sums[0][j], sums[1][j], here[1][j + 1])
                    state[st, 1 - par, x + 2, core(0, j), :] = new_p
                    state[st, 1 - par, x + 2, core(1, j), :] = new_t
                    new[0].append(new_p)
                    new[1].append(new_t)
                for f in range(2):
                    firsts.append(new[f][:2])
                    lasts.append((new[f][-1], new[f][-2]))
            if not last:
                y_message(st, 1 - par, xg, firsts, lasts)
            return 0

        lax.fori_loop(0, XG, rows, 0, unroll=UNROLL // 2)

    base_cell = (lgx * NX) * (ngy * NY) + gy * NY

    def field_halo(n, k):
        if k == 0:
            src, dst = yfield.at[n, :, pl.ds(0, NY)], prow.at[n, 1]
        elif k == 1:
            src, dst = yfield.at[n, :, pl.ds((NX - 1) * NY, NY)], prow.at[n, 0]
        elif k == 2:
            src, dst = ycol.at[n, 0], pcol.at[n, 1]
        else:
            src, dst = ycol.at[n, 1], pcol.at[n, 0]
        return pltpu.make_async_remote_copy(
            src_ref=src,
            dst_ref=dst,
            send_sem=psend.at[n, k],
            recv_sem=precv.at[n, k ^ 1],
            device_id=near[k],
            device_id_type=MESH,
        )

    def repeat(ref, lead, h, value):
        for o in range(SO):
            ref[(*lead, pl.ds(o * NY + h * 8, 8), slice(None))] = value

    def factors(pore, heat, dil, perm):
        store_p = jnp.exp(dil)
        store_t = jnp.exp(0.5 * heat)
        coupling = 0.2 * jnp.tanh(pore)
        inv_p = 1.0 / (store_p + 6.0 * perm)
        inv_t = 1.0 / (store_t + 12.0)
        return (
            perm * inv_p, coupling * inv_p, 2.0 * inv_t, coupling * inv_t,
            store_p * inv_p, inv_p, store_t * inv_t,
        )

    def prepare(n):
        @pl.when(moves)
        def _():
            for d in range(NP):
                forward_copy(n, d).wait_recv()

        for h in range(2):
            whole = [
                regroup([gath[n, d, pl.ds((f * 2 + h) * 8, 8), :] for d in range(NP)], lane_group) for f in range(4)
            ]
            for f in range(4):
                for x in range(NX):
                    yfield[n, f, pl.ds(x * NY + h * 8, 8), :] = whole[f][x]
        for f in range(4):
            for side, y in ((0, 0), (1, NY - 1)):
                ycol[n, side, f] = yfield[n, f, pl.ds(y, NX, stride=NY), :]
        for k in range(4):

            @pl.when(exists[k])
            def _(k=k):
                field_halo(n, k).start()

        def row(x, _):
            for h in range(2):
                values = [yfield[n, f, pl.ds(pl.multiple_of(x * NY + h * 8, 8), 8), :] for f in range(4)]
                for c, value in enumerate(factors(*values)):
                    repeat(crep, (c, x + 1), h, value)
                repeat(crep, (KK, x + 1), h, values[3])
                repeat(prep_pore, (x + 1,), h, values[0])
            return 0

        lax.fori_loop(0, NX, row, 0, unroll=2)

    def complete(n):
        for k in range(4):

            @pl.when(exists[k])
            def _(k=k):
                field_halo(n, k ^ 1).wait_recv()
                field_halo(n, k).wait_send()

        for side, x in ((0, -1), (1, NX)):
            for h in range(2):
                values = [prow[n, side, f, pl.ds(h * 8, 8), :] for f in range(4)]
                for c, value in enumerate(factors(*values)):
                    repeat(crep, (c, x + 1), h, jnp.where(exists[side], value, 0.0))
                repeat(prep_pore, (x + 1,), h, values[0])
            values = [pcol[n, side, f] for f in range(4)]
            for c, value in enumerate(factors(*values)):
                ccol[c, side] = jnp.where(exists[2 + side], value, 0.0)

        def tiles_of(c, x):
            tiles = [crep[c, x + 1, pl.ds(j, 8, stride=NJ), :] for j in range(NJ)]
            for j in range(NJ):
                coef[n, c, x + 1, ext(0, j), :] = tiles[j]
            return tiles

        def spread(x, _):
            for c in range(7):
                tiles = tiles_of(c, x)
                low, high = (jnp.broadcast_to(ccol[c, side, pl.ds(x, 1), :], (8, NZ)) for side in range(2))
                coef[n, c, x + 1, ext(0, -1), :] = before_of(tiles[-1], low)
                coef[n, c, x + 1, ext(0, NJ), :] = after_of(tiles[0], high)
            tiles, up, down = (
                [prep_pore[x + dx, pl.ds(j, 8, stride=NJ), :] for j in range(NJ)] for dx in (1, 0, 2)
            )
            low, high = (jnp.broadcast_to(pcol[n, side, 0, pl.ds(x, 1), :], (8, NZ)) for side in range(2))
            ring = [before_of(tiles[-1], low), *tiles, after_of(tiles[0], high)]
            sums = around(ring, up, down)
            for j in range(NJ):
                perm = crep[KK, x + 1, pl.ds(j, 8, stride=NJ), :]
                coef[n, KK, x + 1, ext(0, j), :] = perm * (sums[j] - 6.0 * tiles[j])
            return 0

        lax.fori_loop(0, NX, spread, 0, unroll=2)
        for c in range(7):
            tiles_of(c, -1)
            tiles_of(c, NX)

    def right_sides(st, par, n):
        source = meta_in[st, n]
        cell = meta_in[st, 3] - (NJ * squarter + base_cell).astype(F32)

        def row(x, reach):
            tiles = [wide(st, par, x, f, reach) for f in range(2)]
            for p in range(NJ + 2 * reach):
                j = p - reach
                at = ext(0, j)
                mine = cell == jnp.asarray(x * (ngy * NY) + j).astype(F32)
                term = jnp.where(mine, source, 0.0)
                right[st, x + 1, at, :] = coef[n, RPC, x + 1, at, :] * tiles[0][p] + coef[n, IP, x + 1, at, :] * term
                right[st, x + 1, ext(1, j), :] = coef[n, RTC, x + 1, at, :] * tiles[1][p]

        def inner(x, _):
            row(x, 1)
            return 0

        lax.fori_loop(0, NX, inner, 0, unroll=2)
        row(-1, 0)
        row(NX, 0)

    def add_gradient(st, par, n):
        weight = meta_in[st, 4]

        def row(x, _):
            for j in range(NJ):
                at = pl.ds(j * 8, 8)
                gacc[x, at, :] += coef[n, KK, x + 1, ext(0, j), :] * (weight * state[st, par, x + 2, core(0, j), :])
            return 0

        lax.fori_loop(0, NX, row, 0, unroll=2)

    def swap_out(k):
        return pltpu.make_async_remote_copy(
            src_ref=outst.at[:, pl.ds(k * NY, NY), :],
            dst_ref=out_ref.at[k // NO, k % NO],
            send_sem=osend.at[k],
            recv_sem=orecv.at[k],
            device_id=partner,
            device_id_type=MESH,
        )

    def keep_out(k):
        return pltpu.make_async_copy(
            outst.at[:, pl.ds(k * NY, NY), :], out_ref.at[k // NO, k % NO], orecv.at[k]
        )

    def finish(st):
        def row(x, _):
            for f in range(2):
                for j in range(NJ):
                    outst[x, pl.ds((f * NO + st * SO) * NY + j, 8, stride=NJ), :] = state[
                        st, ROUNDS % 2, x + 2, core(f, j), :
                    ]
            return 0

        lax.fori_loop(0, NX, row, 0)

        @pl.when(moves)
        def _():
            for k in streams_obs(st):
                swap_out(k).start()

        @pl.when(stays)
        def _():
            for k in streams_obs(st):
                keep_out(k).start()

    def round_of(st, r):
        n, par = NS - 1 - r // 2, r % 2
        wait_halos(st, par)
        if r > 0:
            wait_sent(st, 1 - par)
        fill_edges(st, par)
        if r % 2 == 0:
            right_sides(st, par, n)
        first_sweep(st, par, n)
        second_sweep(st, par, n, r == ROUNDS - 1)
        if r < ROUNDS - 1:
            start_halos(st, 1 - par)
        else:
            finish(st)
        if r % 2 == 1:
            add_gradient(st, 1 - par, n)

    gacc[...] = jnp.zeros(gacc.shape, F32)
    plan = PLAN
    todo = {
        "send": send_saved, "forward": forward, "prepare": prepare, "complete": complete, "set_up": set_up,
    }

    def do(when):
        for what, n in plan.get(when, ()):
            todo[what](n)

    do("start")

    @pl.when(moves)
    def _():
        send_meta().wait()

    for r in range(ROUNDS + LAG * (ST - 1)):
        for st in range(ST):
            if 0 <= r - LAG * st < ROUNDS:
                round_of(st, r - LAG * st)
            do((r, st))
    for st in range(ST):
        wait_sent(st, (ROUNDS - 1) % 2)

    for x in range(NX):
        for j in range(NJ):
            total = gacc[x, pl.ds(j * 8, 8), :]
            for o in range(1, SO):
                total = total + pltpu.roll(gacc[x, pl.ds(j * 8, 8), :], NQ * o, 0)
            gsum[x, pl.ds(j, 8, stride=NJ), :] = total
    for h in range(2):
        whole = [gsum[x, pl.ds(h * 8, 8), :] for x in range(NX)]
        for d, tile in enumerate(regroup(whole, lane_group)):
            gpack[d, pl.ds(h * 8, 8), :] = tile

            @pl.when(jnp.logical_and(stays, obs == d))
            def _(tile=tile, h=h):
                gred[lobs, pl.ds(h * 8, 8), :] = tile

    def reduce_copy(d):
        return pltpu.make_async_remote_copy(
            src_ref=gpack.at[d],
            dst_ref=gred.at[lobs],
            send_sem=rsend.at[d],
            recv_sem=rrecv.at[lobs],
            device_id=(d, lgx, gy),
            device_id_type=MESH,
        )

    for d in range(NP):

        @pl.when(jnp.logical_not(jnp.logical_and(stays, obs == d)))
        def _(d=d):
            reduce_copy(d).start()

    for d in range(NP):

        @pl.when(jnp.logical_not(is_me(d)))
        def _(d=d):
            pltpu.make_async_remote_copy(
                src_ref=gpack.at[d],
                dst_ref=gred.at[d],
                send_sem=rsend.at[d],
                recv_sem=rrecv.at[d],
                device_id=partner,
                device_id_type=MESH,
            ).wait_recv()

    for h in range(2):
        total = gred[0, pl.ds(h * 8, 8), :]
        for d in range(1, NP):
            total = total + gred[d, pl.ds(h * 8, 8), :]
        for x in range(NX):
            turned = pltpu.roll(total, NZ - LP * x, 1) if x else total
            grad_ref[x, pl.ds(h * 8, 8), :] = turned

    for d in range(NP):

        @pl.when(jnp.logical_not(jnp.logical_and(stays, obs == d)))
        def _(d=d):
            reduce_copy(d).wait_send()

    for n in range(NS):
        for zt in range(4):

            @pl.when(jnp.logical_not(jnp.logical_and(stays, zh == zt)))
            def _(n=n, zt=zt):
                gather_copy(n, zt).wait_send()

        @pl.when(stays)
        def _(n=n):
            for d in range(NP):
                forward_copy(n, d).wait_send()

    @pl.when(moves)
    def _():
        for k in range(2 * NO):
            swap_out(k).wait()

    @pl.when(stays)
    def _():
        for k in range(2 * NO):
            keep_out(k).wait()


def local(*args):
    hbm = pl.BlockSpec(memory_space=pl.ANY)
    vmem = pl.BlockSpec(memory_space=pltpu.VMEM)
    smem = pl.BlockSpec(memory_space=pltpu.SMEM)
    dma = pltpu.SemaphoreType.DMA
    costates, gradient = pl.pallas_call(
        kernel,
        out_shape=(
            jax.ShapeDtypeStruct((2, NO, NX, NY, NZ), F32),
            jax.ShapeDtypeStruct((NX, NY, NZ), F32),
        ),
        in_specs=[hbm, hbm, hbm, hbm, hbm, vmem, smem, smem],
        out_specs=(hbm, vmem),
        scratch_shapes=[
            pltpu.VMEM((NS, 4, NX, NY, LP), F32),
            pltpu.VMEM((NS, 64, NZ), F32),
            pltpu.VMEM((NS, NP, 64, NZ), F32),
            pltpu.VMEM((NX, 2 * NO * NY, NZ), F32),
            pltpu.VMEM((ST, 5, 8, NZ), F32),
            pltpu.VMEM((ST, 5, 8, NZ), F32),
            pltpu.VMEM((ST, 2, NX + 4, ROWS, NZ), F32),
            pltpu.VMEM((ST, NX + 2, 2 * NE * 8, NZ), F32),
            pltpu.VMEM((ST, NX + 2, 2, 4, 8, NZ), F32),
            pltpu.VMEM((ST, 2, 2, 2, XG * 8, NZ), F32),
            pltpu.VMEM((ST, 2, 2, 2, XG * 8, NZ), F32),
            pltpu.VMEM((ST, 2, 4, 8, NZ), F32),
            pltpu.VMEM((NS, 8, NX + 2, NE * 8, NZ), F32),
            pltpu.VMEM((8, NX + 2, SO * NY, NZ), F32),
            pltpu.VMEM((7, 2, 8, NZ), F32),
            pltpu.VMEM((NX + 2, SO * NY, NZ), F32),
            pltpu.VMEM((NS, 4, NX * NY, NZ), F32),
            pltpu.VMEM((NS, 2, 4, 8, NZ), F32),
            pltpu.VMEM((NS, 2, 4, NY, NZ), F32),
            pltpu.VMEM((NS, 2, 4, 8, NZ), F32),
            pltpu.VMEM((ST, NX + 2, 2 * NE * 8, NZ), F32),
            pltpu.VMEM((NX, NJ * 8, NZ), F32),
            pltpu.VMEM((NX, 8 * NJ, NZ), F32),
            pltpu.VMEM((NP, NY, NZ), F32),
            pltpu.VMEM((NP, NY, NZ), F32),
            pltpu.VMEM((NX, 2 * NO * NY, NZ), F32),
            dma((NS, 4)),
            dma((NS, 4)),
            dma((NS, NP)),
            dma((NS, NP)),
            dma((2 * NO,)),
            dma((2 * NO,)),
            dma((2,)),
            dma((ST, 2, 4)),
            dma((ST, 2, 4)),
            dma((ST, 2, 4)),
            dma((ST, 2, 4)),
            dma((NS, 4)),
            dma((NS, 4)),
            dma((2 * NO,)),
            dma((2 * NO,)),
            dma((NP,)),
            dma((NP,)),
        ],
        compiler_params=pltpu.CompilerParams(
            collective_id=0, has_side_effects=True, vmem_limit_bytes=67043328
        ),
    )(*args)
    return costates, gradient[:, :, :LP]


def solution(mesh):
    return jax.shard_map(
        local,
        mesh=mesh,
        in_specs=(
            P(None, "obs", "gx", "gy", None),
            P(None, "gx", "gy", "obs"),
            P(None, "gx", "gy", "obs"),
            P(None, "gx", "gy", "obs"),
            P(None, "gx", "gy", "obs"),
            P(None, "obs", None),
            P("obs"),
            P("obs"),
        ),
        out_specs=(P(None, "obs", "gx", "gy", None), P("gx", "gy", "obs")),
        check_vma=False,
    )
```

```python
import functools

import jax
import jax.numpy as jnp
from jax import lax
from jax.experimental import pallas as pl
from jax.experimental.pallas import tpu as pltpu
from jax.sharding import PartitionSpec as P

MESH = pl.DeviceIdType.MESH
F32 = jnp.float32
ITERS = 4
LAG = 0
UNROLL = 8
NX, NY, NZ = 8, 16, 128
NS = 3
NO = 4
NP = 8
LP = NZ // NP
SO = 2
ST = NO // SO
NQ = 8 // SO
NJ = NY // NQ
NG = NQ // 2
XG = NX // NG
ROWS = 2 * NJ * 8
NE = NJ + 2
ROUNDS = NS * ITERS // 2
AP, BP, AT, BT, RPC, IP, RTC, KK = range(8)


PLAN = {
    "start": (("forward", 2), ("send", 1), ("prepare", 2), ("set_up", 0), ("set_up", 1), ("complete", 2)),
    (0, 0): (("forward", 1), ("send", 0)),
    (1, 0): (("prepare", 1), ("forward", 0)),
    (1, 1): (("complete", 1),),
    (2, 1): (("prepare", 0),),
    (3, 1): (("complete", 0),),
}


def role(obs, gx):
    return 2 * (obs // 2) + gx % 2, 2 * (gx // 2) + obs % 2


def regroup(tiles, lane_group):
    turned = [pltpu.roll(t, LP * d, 1) if d else t for d, t in enumerate(tiles)]
    outs = []
    for x in range(NP):
        mixed = turned[(NP - 1 - x) % NP]
        for g in range(NP - 1):
            mixed = jnp.where(lane_group == g, turned[(g - x) % NP], mixed)
        outs.append(pltpu.roll(mixed, NZ - LP * x, 1) if x else mixed)
    return outs


def kernel(
    cost_ref, pore_ref, heat_ref, dil_ref, cond_ref, resid_ref, pos_ref, wgt_ref,
    out_ref, grad_ref,
    saved, pack, gath, raw, meta, meta_in, state, mid, edge, ysend, yrecv, corner,
    coef, crep, ccol, prep_pore, yfield, ycol, prow, pcol, right, gacc, gsum, gpack, gred, outst,
    load_sem, gsend, grecv, gfwd, ssend, srecv, msem, hsend, hrecv, csend, crecv, psend, precv, osend, orecv, rsend, rrecv,
):
    obs, gx, gy = lax.axis_index("obs"), lax.axis_index("gx"), lax.axis_index("gy")
    lobs, lgx = role(obs, gx)
    stays = jnp.logical_and(lobs == obs, lgx == gx)
    moves = jnp.logical_not(stays)
    zh, yy = obs // 2, gx // 2
    ngx, ngy = lax.axis_size("gx"), lax.axis_size("gy")

    lane = lax.broadcasted_iota(jnp.int32, (8, NZ), 1)
    sub = lax.broadcasted_iota(jnp.int32, (8, NZ), 0)
    lane_group = lane // LP
    first_lane, last_lane = lane == 0, lane == NZ - 1

    exists = (lgx > 0, lgx < ngx - 1, gy > 0, gy < ngy - 1)
    xm = role(lobs, jnp.maximum(lgx - 1, 0))
    xp = role(lobs, jnp.minimum(lgx + 1, ngx - 1))
    near = (
        (xm[0], xm[1], gy),
        (xp[0], xp[1], gy),
        (obs, gx, jnp.maximum(gy - 1, 0)),
        (obs, gx, jnp.minimum(gy + 1, ngy - 1)),
    )
    slant_exists = [jnp.logical_and(exists[cx], exists[2 + cy]) for cx in range(2) for cy in range(2)]
    slant = [(near[cx][0], near[cx][1], near[2 + cy][2]) for cx in range(2) for cy in range(2)]
    partner = (lobs, lgx, gy)

    fields = (pore_ref, heat_ref, dil_ref, cond_ref)

    def load(n, f):
        return pltpu.make_async_copy(fields[f].at[n], saved.at[n, f], load_sem.at[n, f])

    for n in range(NS - 1, -1, -1):
        for f in range(4):
            load(n, f).start()

    zero = jnp.zeros((8, NZ), F32)
    for st in range(ST):
        for par in range(2):
            for row in (0, 1, NX + 2, NX + 3):
                state[st, par, row] = jnp.zeros((ROWS, NZ), F32)
    yrecv[...] = jnp.zeros(yrecv.shape, F32)
    corner[...] = jnp.zeros(corner.shape, F32)
    prow[...] = jnp.zeros(prow.shape, F32)
    pcol[...] = jnp.zeros(pcol.shape, F32)

    barrier = pltpu.get_barrier_semaphore()
    for zz in range(4):
        for core in range(2):
            for low in range(2):
                there = (2 * zz + core, 2 * yy + low, gy)

                @pl.when(jnp.logical_or(there[0] != obs, there[1] != gx))
                def _(there=there):
                    pl.semaphore_signal(barrier, inc=1, device_id=there, device_id_type=MESH)

    for k in range(4):

        @pl.when(exists[k])
        def _(k=k):
            pl.semaphore_signal(barrier, inc=1, device_id=near[k], device_id_type=MESH)

        @pl.when(slant_exists[k])
        def _(k=k):
            pl.semaphore_signal(barrier, inc=1, device_id=slant[k], device_id_type=MESH)

    count = 15
    for k in range(4):
        count = count + exists[k].astype(jnp.int32) + slant_exists[k].astype(jnp.int32)
    pl.semaphore_wait(barrier, count)

    srow = sub // NQ
    squarter = sub % NQ
    for st in range(ST):
        for n in range(NS):
            tile = zero
            for o in range(SO):
                k = st * SO + o
                tile = jnp.where(srow == o, jnp.broadcast_to(resid_ref[n, k : k + 1, :], (8, NZ)), tile)
            meta[st, n] = tile
        pos = jnp.zeros((8, NZ), jnp.int32)
        wgt = jnp.zeros((8, NZ), jnp.int32)
        for o in range(SO):
            pos = jnp.where(srow == o, pos_ref[st * SO + o], pos)
            wgt = jnp.where(srow == o, wgt_ref[st * SO + o], wgt)
        meta[st, 3] = pos.astype(F32)
        meta[st, 4] = wgt.astype(F32)

    def gather_copy(n, zt):
        return pltpu.make_async_remote_copy(
            src_ref=pack.at[n],
            dst_ref=gath.at[n, obs],
            send_sem=gsend.at[n, zt],
            recv_sem=grecv.at[n, obs],
            device_id=(2 * zt + gx % 2, gx, gy),
            device_id_type=MESH,
        )

    zl = gx % 2
    onward = (2 * lax.rem(zh + 3 + 2 * zl, 4) + zl, 2 * yy + 1 - zl, gy)

    def forward_copy(n, d):
        return pltpu.make_async_remote_copy(
            src_ref=gath.at[n, d],
            dst_ref=gath.at[n, d],
            send_sem=gfwd.at[n, d],
            recv_sem=grecv.at[n, d],
            device_id=onward,
            device_id_type=MESH,
        )

    def forward(n):
        @pl.when(stays)
        def _():
            for off in (0, 1, 3, 2):
                for core in range(2):
                    d = 2 * lax.rem(zh + off, 4) + core
                    if off == 0:

                        @pl.when(obs != d)
                        def _(d=d):
                            forward_copy(n, d).wait_recv()

                    else:
                        forward_copy(n, d).wait_recv()
                    forward_copy(n, d).start()

    def is_me(target):
        return jnp.logical_and(stays, lobs == target)

    def send_saved(n):
        for f in range(4):
            load(n, f).wait()
        for f in range(4):
            for h in range(2):
                packed = saved_tile(n, f, 0, h)
                for x in range(1, NX):
                    packed = jnp.where(
                        lane_group == x, pltpu.roll(saved_tile(n, f, x, h), LP * x, 1), packed
                    )
                pack[n, pl.ds((f * 2 + h) * 8, 8), :] = packed

                @pl.when(stays)
                def _(packed=packed, f=f, h=h):
                    gath[n, obs, pl.ds((f * 2 + h) * 8, 8), :] = packed

        for zt in range(4):

            @pl.when(jnp.logical_not(jnp.logical_and(stays, zh == zt)))
            def _(zt=zt):
                gather_copy(n, zt).start()

    def saved_tile(n, f, x, h):
        piece = saved[n, f, x, pl.ds(h * 8, 8), :]
        return jnp.concatenate([piece, jnp.zeros((8, NZ - LP), F32)], axis=1)

    def swap_in(k):
        return pltpu.make_async_remote_copy(
            src_ref=cost_ref.at[k // NO, k % NO],
            dst_ref=raw.at[:, pl.ds(k * NY, NY), :],
            send_sem=ssend.at[k],
            recv_sem=srecv.at[k],
            device_id=partner,
            device_id_type=MESH,
        )

    def keep_in(k):
        return pltpu.make_async_copy(
            cost_ref.at[k // NO, k % NO], raw.at[:, pl.ds(k * NY, NY), :], srecv.at[k]
        )

    def send_meta():
        return pltpu.make_async_remote_copy(
            src_ref=meta, dst_ref=meta_in, send_sem=msem.at[0], recv_sem=msem.at[1], device_id=partner, device_id_type=MESH
        )

    def streams_obs(st):
        return [f * NO + st * SO + o for f in range(2) for o in range(SO)]

    send_saved(NS - 1)

    @pl.when(moves)
    def _():
        send_meta().start()
        for st in range(ST):
            for k in streams_obs(st):
                swap_in(k).start()

    @pl.when(stays)
    def _():
        for st in range(ST):
            for k in streams_obs(st):
                keep_in(k).start()
        meta_in[...] = meta[...]

    def halo(st, par, k):
        if k == 0:
            src, dst = state.at[st, par, pl.ds(2, 2)], state.at[st, par, pl.ds(NX + 2, 2)]
        elif k == 1:
            src, dst = state.at[st, par, pl.ds(NX, 2)], state.at[st, par, pl.ds(0, 2)]
        elif k == 2:
            src, dst = ysend.at[st, par, 0], yrecv.at[st, par, 1]
        else:
            src, dst = ysend.at[st, par, 1], yrecv.at[st, par, 0]
        return pltpu.make_async_remote_copy(
            src_ref=src,
            dst_ref=dst,
            send_sem=hsend.at[st, par, k],
            recv_sem=hrecv.at[st, par, k ^ 1],
            device_id=near[k],
            device_id_type=MESH,
        )

    def corner_copy(st, par, k):
        cx, cy = k // 2, k % 2
        return pltpu.make_async_remote_copy(
            src_ref=ysend.at[st, par, cy, 0, pl.ds((XG - 1) * 8 if cx else 0, 8)],
            dst_ref=corner.at[st, par, 3 - k],
            send_sem=csend.at[st, par, k],
            recv_sem=crecv.at[st, par, 3 - k],
            device_id=slant[k],
            device_id_type=MESH,
        )

    def start_halos(st, par):
        for k in range(4):

            @pl.when(slant_exists[k])
            def _(k=k):
                corner_copy(st, par, k).start()

        for k in range(4):

            @pl.when(exists[k])
            def _(k=k):
                halo(st, par, k).start()

    def wait_sent(st, par):
        for k in range(4):

            @pl.when(exists[k])
            def _(k=k):
                halo(st, par, k).wait_send()

            @pl.when(slant_exists[k])
            def _(k=k):
                corner_copy(st, par, k).wait_send()

    def wait_halos(st, par):
        for k in range(4):

            @pl.when(exists[k])
            def _(k=k):
                halo(st, par, k ^ 1).wait_recv()

            @pl.when(slant_exists[k])
            def _(k=k):
                corner_copy(st, par, 3 - k).wait_recv()

    def y_message(st, par, xg, firsts, lasts):
        for col in range(2):
            low, high = firsts[0][col], pltpu.roll(lasts[0][col], (9 - NQ) % 8, 0)
            for i in range(1, NQ):
                low = jnp.where(squarter == i, pltpu.roll(firsts[i][col], i, 0), low)
                turned = lasts[i][col] if i == NQ - 1 else pltpu.roll(lasts[i][col], (9 + i - NQ) % 8, 0)
                high = jnp.where(squarter == i, turned, high)
            ysend[st, par, 0, col, pl.ds(xg * 8, 8), :] = low
            ysend[st, par, 1, col, pl.ds(xg * 8, 8), :] = high

    def core(f, j):
        return pl.ds((f * NJ + j) * 8, 8)

    def ext(f, j):
        return pl.ds((f * NE + j + 1) * 8, 8)

    def set_up(st):
        @pl.when(moves)
        def _():
            for k in streams_obs(st):
                swap_in(k).wait()

        @pl.when(stays)
        def _():
            for k in streams_obs(st):
                keep_in(k).wait()

        def first_rows(xg, _):
            firsts, lasts = [], []
            for g in range(NG):
                x = xg + g * XG
                for f in range(2):
                    start = (f * NO + st * SO) * NY
                    tiles = [raw[x, pl.ds(start + j, 8, stride=NJ), :] for j in range(NJ)]
                    for j in range(NJ):
                        state[st, 0, x + 2, core(f, j), :] = tiles[j]
                    firsts.append(tiles[:2])
                    lasts.append((tiles[-1], tiles[-2]))
            y_message(st, 0, xg, firsts, lasts)
            return 0

        lax.fori_loop(0, XG, first_rows, 0)
        start_halos(st, 0)

    def around(tiles, up, down):
        sums = []
        for j, (above, below) in enumerate(zip(up, down)):
            here = tiles[j + 1]
            total = above + below + tiles[j] + tiles[j + 2]
            deep = jnp.where(first_lane, 0.0, pltpu.roll(here, 1, 1))
            shallow = jnp.where(last_lane, 0.0, pltpu.roll(here, NZ - 1, 1))
            sums.append(total + deep + shallow)
        return sums

    def before_of(inner, outside):
        return jnp.where(squarter == 0, outside, pltpu.roll(inner, 1, 0))

    def after_of(inner, outside):
        return jnp.where(squarter == NQ - 1, outside, pltpu.roll(inner, 7, 0))

    def slot_low(tile, i):
        return pltpu.roll(tile, 8 - i, 0) if i else tile

    def slot_high(tile, i):
        return pltpu.roll(tile, NQ - 1 - i, 0) if i < NQ - 1 else tile

    def fill_edges(st, par):
        def rows(xg, _):
            lows = [yrecv[st, par, 0, col, pl.ds(xg * 8, 8), :] for col in range(2)]
            highs = [yrecv[st, par, 1, col, pl.ds(xg * 8, 8), :] for col in range(2)]
            for g in range(NG):
                x = xg + g * XG
                for f in range(2):
                    i = 2 * g + f
                    for col in range(2):
                        inner = state[st, par, x + 2, core(f, NJ - 1 - col), :]
                        edge[st, x + 1, f, 1 - col] = before_of(inner, slot_low(lows[col], i))
                        inner = state[st, par, x + 2, core(f, col), :]
                        edge[st, x + 1, f, 2 + col] = after_of(inner, slot_high(highs[col], i))
            return 0

        lax.fori_loop(0, XG, rows, 0, unroll=2)
        for cx, x, g in ((0, -1, NG - 1), (1, NX, 0)):
            for f in range(2):
                i = 2 * g + f
                inner = state[st, par, x + 2, core(f, NJ - 1), :]
                edge[st, x + 1, f, 1] = before_of(inner, slot_low(corner[st, par, 2 * cx], i))
                inner = state[st, par, x + 2, core(f, 0), :]
                edge[st, x + 1, f, 2] = after_of(inner, slot_high(corner[st, par, 2 * cx + 1], i))

    def wide(st, par, x, f, reach):
        tiles = [state[st, par, x + 2, core(f, j), :] for j in range(NJ)]
        low = [edge[st, x + 1, f, e] for e in range(2 - reach, 2)]
        high = [edge[st, x + 1, f, e] for e in range(2, 2 + reach)]
        return low + tiles + high

    def relaxed(st, n, x, j, near_p, near_t, old_t):
        at, at_t = ext(0, j), ext(1, j)
        new_p = right[st, x + 1, at, :] + coef[n, AP, x + 1, at, :] * near_p + coef[n, BP, x + 1, at, :] * old_t
        new_t = right[st, x + 1, at_t, :] + coef[n, AT, x + 1, at, :] * near_t + coef[n, BT, x + 1, at, :] * new_p
        return new_p, new_t

    def first_sweep(st, par, n):
        def row(x, reach):
            here, sums = [], []
            for f in range(2):
                tiles = wide(st, par, x, f, reach + 1)
                up, down = wide(st, par, x - 1, f, reach), wide(st, par, x + 1, f, reach)
                here.append(tiles)
                sums.append(around(tiles, up, down))
            for p in range(NJ + 2 * reach):
                j = p - reach
                new_p, new_t = relaxed(st, n, x, j, sums[0][p], sums[1][p], here[1][p + 1])
                mid[st, x + 1, ext(0, j), :] = new_p
                mid[st, x + 1, ext(1, j), :] = new_t

        def inner(x, _):
            row(x, 1)
            return 0

        lax.fori_loop(0, NX, inner, 0, unroll=UNROLL)
        row(-1, 0)
        row(NX, 0)

    def second_sweep(st, par, n, last):
        def rows(xg, _):
            firsts, lasts = [], []
            for g in range(NG):
                x = xg + g * XG
                here, sums = [], []
                for f in range(2):
                    tiles = [mid[st, x + 1, ext(f, j), :] for j in range(-1, NJ + 1)]
                    up = [mid[st, x, ext(f, j), :] for j in range(NJ)]
                    down = [mid[st, x + 2, ext(f, j), :] for j in range(NJ)]
                    here.append(tiles)
                    sums.append(around(tiles, up, down))
                new = [[], []]
                for j in range(NJ):
                    new_p, new_t = relaxed(st, n, x, j, sums[0][j], sums[1][j], here[1][j + 1])
                    state[st, 1 - par, x + 2, core(0, j), :] = new_p
                    state[st, 1 - par, x + 2, core(1, j), :] = new_t
                    new[0].append(new_p)
                    new[1].append(new_t)
                for f in range(2):
                    firsts.append(new[f][:2])
                    lasts.append((new[f][-1], new[f][-2]))
            if not last:
                y_message(st, 1 - par, xg, firsts, lasts)
            return 0

        lax.fori_loop(0, XG, rows, 0, unroll=UNROLL // 2)

    base_cell = (lgx * NX) * (ngy * NY) + gy * NY

    def field_halo(n, k):
        if k == 0:
            src, dst = yfield.at[n, :, pl.ds(0, NY)], prow.at[n, 1]
        elif k == 1:
            src, dst = yfield.at[n, :, pl.ds((NX - 1) * NY, NY)], prow.at[n, 0]
        elif k == 2:
            src, dst = ycol.at[n, 0], pcol.at[n, 1]
        else:
            src, dst = ycol.at[n, 1], pcol.at[n, 0]
        return pltpu.make_async_remote_copy(
            src_ref=src,
            dst_ref=dst,
            send_sem=psend.at[n, k],
            recv_sem=precv.at[n, k ^ 1],
            device_id=near[k],
            device_id_type=MESH,
        )

    def repeat(ref, lead, h, value):
        for o in range(SO):
            ref[(*lead, pl.ds(o * NY + h * 8, 8), slice(None))] = value

    def factors(pore, heat, dil, perm):
        store_p = jnp.exp(dil)
        store_t = jnp.exp(0.5 * heat)
        coupling = 0.2 * jnp.tanh(pore)
        inv_p = 1.0 / (store_p + 6.0 * perm)
        inv_t = 1.0 / (store_t + 12.0)
        return (
            perm * inv_p, coupling * inv_p, 2.0 * inv_t, coupling * inv_t,
            store_p * inv_p, inv_p, store_t * inv_t,
        )

    def prepare(n):
        @pl.when(moves)
        def _():
            for d in range(NP):
                forward_copy(n, d).wait_recv()

        for h in range(2):
            whole = [
                regroup([gath[n, d, pl.ds((f * 2 + h) * 8, 8), :] for d in range(NP)], lane_group) for f in range(4)
            ]
            for f in range(4):
                for x in range(NX):
                    yfield[n, f, pl.ds(x * NY + h * 8, 8), :] = whole[f][x]
        for f in range(4):
            for side, y in ((0, 0), (1, NY - 1)):
                ycol[n, side, f] = yfield[n, f, pl.ds(y, NX, stride=NY), :]
        for k in range(4):

            @pl.when(exists[k])
            def _(k=k):
                field_halo(n, k).start()

        def row(x, _):
            for h in range(2):
                values = [yfield[n, f, pl.ds(pl.multiple_of(x * NY + h * 8, 8), 8), :] for f in range(4)]
                for c, value in enumerate(factors(*values)):
                    repeat(crep, (c, x + 1), h, value)
                repeat(crep, (KK, x + 1), h, values[3])
                repeat(prep_pore, (x + 1,), h, values[0])
            return 0

        lax.fori_loop(0, NX, row, 0, unroll=2)

    def complete(n):
        for k in range(4):

            @pl.when(exists[k])
            def _(k=k):
                field_halo(n, k ^ 1).wait_recv()
                field_halo(n, k).wait_send()

        for side, x in ((0, -1), (1, NX)):
            for h in range(2):
                values = [prow[n, side, f, pl.ds(h * 8, 8), :] for f in range(4)]
                for c, value in enumerate(factors(*values)):
                    repeat(crep, (c, x + 1), h, jnp.where(exists[side], value, 0.0))
                repeat(prep_pore, (x + 1,), h, values[0])
            values = [pcol[n, side, f] for f in range(4)]
            for c, value in enumerate(factors(*values)):
                ccol[c, side] = jnp.where(exists[2 + side], value, 0.0)

        def tiles_of(c, x):
            tiles = [crep[c, x + 1, pl.ds(j, 8, stride=NJ), :] for j in range(NJ)]
            for j in range(NJ):
                coef[n, c, x + 1, ext(0, j), :] = tiles[j]
            return tiles

        def spread(x, _):
            for c in range(7):
                tiles = tiles_of(c, x)
                low, high = (jnp.broadcast_to(ccol[c, side, pl.ds(x, 1), :], (8, NZ)) for side in range(2))
                coef[n, c, x + 1, ext(0, -1), :] = before_of(tiles[-1], low)
                coef[n, c, x + 1, ext(0, NJ), :] = after_of(tiles[0], high)
            tiles, up, down = (
                [prep_pore[x + dx, pl.ds(j, 8, stride=NJ), :] for j in range(NJ)] for dx in (1, 0, 2)
            )
            low, high = (jnp.broadcast_to(pcol[n, side, 0, pl.ds(x, 1), :], (8, NZ)) for side in range(2))
            ring = [before_of(tiles[-1], low), *tiles, after_of(tiles[0], high)]
            sums = around(ring, up, down)
            for j in range(NJ):
                perm = crep[KK, x + 1, pl.ds(j, 8, stride=NJ), :]
                coef[n, KK, x + 1, ext(0, j), :] = perm * (sums[j] - 6.0 * tiles[j])
            return 0

        lax.fori_loop(0, NX, spread, 0, unroll=2)
        for c in range(7):
            tiles_of(c, -1)
            tiles_of(c, NX)

    def right_sides(st, par, n):
        source = meta_in[st, n]
        cell = meta_in[st, 3] - (NJ * squarter + base_cell).astype(F32)

        def row(x, reach):
            tiles = [wide(st, par, x, f, reach) for f in range(2)]
            for p in range(NJ + 2 * reach):
                j = p - reach
                at = ext(0, j)
                mine = cell == jnp.asarray(x * (ngy * NY) + j).astype(F32)
                term = jnp.where(mine, source, 0.0)
                right[st, x + 1, at, :] = coef[n, RPC, x + 1, at, :] * tiles[0][p] + coef[n, IP, x + 1, at, :] * term
                right[st, x + 1, ext(1, j), :] = coef[n, RTC, x + 1, at, :] * tiles[1][p]

        def inner(x, _):
            row(x, 1)
            return 0

        lax.fori_loop(0, NX, inner, 0, unroll=2)
        row(-1, 0)
        row(NX, 0)

    def add_gradient(st, par, n):
        weight = meta_in[st, 4]

        def row(x, _):
            for j in range(NJ):
                at = pl.ds(j * 8, 8)
                gacc[x, at, :] += coef[n, KK, x + 1, ext(0, j), :] * (weight * state[st, par, x + 2, core(0, j), :])
            return 0

        lax.fori_loop(0, NX, row, 0, unroll=2)

    def swap_out(k):
        return pltpu.make_async_remote_copy(
            src_ref=outst.at[:, pl.ds(k * NY, NY), :],
            dst_ref=out_ref.at[k // NO, k % NO],
            send_sem=osend.at[k],
            recv_sem=orecv.at[k],
            device_id=partner,
            device_id_type=MESH,
        )

    def keep_out(k):
        return pltpu.make_async_copy(
            outst.at[:, pl.ds(k * NY, NY), :], out_ref.at[k // NO, k % NO], orecv.at[k]
        )

    def finish(st):
        def row(x, _):
            for f in range(2):
                for j in range(NJ):
                    outst[x, pl.ds((f * NO + st * SO) * NY + j, 8, stride=NJ), :] = state[
                        st, ROUNDS % 2, x + 2, core(f, j), :
                    ]
            return 0

        lax.fori_loop(0, NX, row, 0)

        @pl.when(moves)
        def _():
            for k in streams_obs(st):
                swap_out(k).start()

        @pl.when(stays)
        def _():
            for k in streams_obs(st):
                keep_out(k).start()

    def round_of(st, r):
        n, par = NS - 1 - r // 2, r % 2
        wait_halos(st, par)
        if r > 0:
            wait_sent(st, 1 - par)
        fill_edges(st, par)
        if r % 2 == 0:
            right_sides(st, par, n)
        first_sweep(st, par, n)
        second_sweep(st, par, n, r == ROUNDS - 1)
        if r < ROUNDS - 1:
            start_halos(st, 1 - par)
        elif st < ST - 1:
            finish(st)
        if r % 2 == 1:
            add_gradient(st, 1 - par, n)

    gacc[...] = jnp.zeros(gacc.shape, F32)
    plan = PLAN
    todo = {
        "send": send_saved, "forward": forward, "prepare": prepare, "complete": complete, "set_up": set_up,
    }

    def do(when):
        for what, n in plan.get(when, ()):
            todo[what](n)

    do("start")

    @pl.when(moves)
    def _():
        send_meta().wait()

    for r in range(ROUNDS + LAG * (ST - 1)):
        for st in range(ST):
            if 0 <= r - LAG * st < ROUNDS:
                round_of(st, r - LAG * st)
            do((r, st))
    for x in range(NX):
        for j in range(NJ):
            total = gacc[x, pl.ds(j * 8, 8), :]
            for o in range(1, SO):
                total = total + pltpu.roll(gacc[x, pl.ds(j * 8, 8), :], NQ * o, 0)
            gsum[x, pl.ds(j, 8, stride=NJ), :] = total
    for h in range(2):
        whole = [gsum[x, pl.ds(h * 8, 8), :] for x in range(NX)]
        for d, tile in enumerate(regroup(whole, lane_group)):
            gpack[d, pl.ds(h * 8, 8), :] = tile

            @pl.when(jnp.logical_and(stays, obs == d))
            def _(tile=tile, h=h):
                gred[lobs, pl.ds(h * 8, 8), :] = tile

    def reduce_copy(d):
        return pltpu.make_async_remote_copy(
            src_ref=gpack.at[d],
            dst_ref=gred.at[lobs],
            send_sem=rsend.at[d],
            recv_sem=rrecv.at[lobs],
            device_id=(d, lgx, gy),
            device_id_type=MESH,
        )

    for d in range(NP):

        @pl.when(jnp.logical_not(jnp.logical_and(stays, obs == d)))
        def _(d=d):
            reduce_copy(d).start()

    finish(ST - 1)
    for st in range(ST):
        wait_sent(st, (ROUNDS - 1) % 2)

    for d in range(NP):

        @pl.when(jnp.logical_not(is_me(d)))
        def _(d=d):
            pltpu.make_async_remote_copy(
                src_ref=gpack.at[d],
                dst_ref=gred.at[d],
                send_sem=rsend.at[d],
                recv_sem=rrecv.at[d],
                device_id=partner,
                device_id_type=MESH,
            ).wait_recv()

    for h in range(2):
        total = gred[0, pl.ds(h * 8, 8), :]
        for d in range(1, NP):
            total = total + gred[d, pl.ds(h * 8, 8), :]
        for x in range(NX):
            turned = pltpu.roll(total, NZ - LP * x, 1) if x else total
            grad_ref[x, pl.ds(h * 8, 8), :] = turned

    for d in range(NP):

        @pl.when(jnp.logical_not(jnp.logical_and(stays, obs == d)))
        def _(d=d):
            reduce_copy(d).wait_send()

    for n in range(NS):
        for zt in range(4):

            @pl.when(jnp.logical_not(jnp.logical_and(stays, zh == zt)))
            def _(n=n, zt=zt):
                gather_copy(n, zt).wait_send()

        @pl.when(stays)
        def _(n=n):
            for d in range(NP):
                forward_copy(n, d).wait_send()

    @pl.when(moves)
    def _():
        for k in range(2 * NO):
            swap_out(k).wait()

    @pl.when(stays)
    def _():
        for k in range(2 * NO):
            keep_out(k).wait()


def local(*args):
    hbm = pl.BlockSpec(memory_space=pl.ANY)
    vmem = pl.BlockSpec(memory_space=pltpu.VMEM)
    smem = pl.BlockSpec(memory_space=pltpu.SMEM)
    dma = pltpu.SemaphoreType.DMA
    costates, gradient = pl.pallas_call(
        kernel,
        out_shape=(
            jax.ShapeDtypeStruct((2, NO, NX, NY, NZ), F32),
            jax.ShapeDtypeStruct((NX, NY, NZ), F32),
        ),
        in_specs=[hbm, hbm, hbm, hbm, hbm, vmem, smem, smem],
        out_specs=(hbm, vmem),
        scratch_shapes=[
            pltpu.VMEM((NS, 4, NX, NY, LP), F32),
            pltpu.VMEM((NS, 64, NZ), F32),
            pltpu.VMEM((NS, NP, 64, NZ), F32),
            pltpu.VMEM((NX, 2 * NO * NY, NZ), F32),
            pltpu.VMEM((ST, 5, 8, NZ), F32),
            pltpu.VMEM((ST, 5, 8, NZ), F32),
            pltpu.VMEM((ST, 2, NX + 4, ROWS, NZ), F32),
            pltpu.VMEM((ST, NX + 2, 2 * NE * 8, NZ), F32),
            pltpu.VMEM((ST, NX + 2, 2, 4, 8, NZ), F32),
            pltpu.VMEM((ST, 2, 2, 2, XG * 8, NZ), F32),
            pltpu.VMEM((ST, 2, 2, 2, XG * 8, NZ), F32),
            pltpu.VMEM((ST, 2, 4, 8, NZ), F32),
            pltpu.VMEM((NS, 8, NX + 2, NE * 8, NZ), F32),
            pltpu.VMEM((8, NX + 2, SO * NY, NZ), F32),
            pltpu.VMEM((7, 2, 8, NZ), F32),
            pltpu.VMEM((NX + 2, SO * NY, NZ), F32),
            pltpu.VMEM((NS, 4, NX * NY, NZ), F32),
            pltpu.VMEM((NS, 2, 4, 8, NZ), F32),
            pltpu.VMEM((NS, 2, 4, NY, NZ), F32),
            pltpu.VMEM((NS, 2, 4, 8, NZ), F32),
            pltpu.VMEM((ST, NX + 2, 2 * NE * 8, NZ), F32),
            pltpu.VMEM((NX, NJ * 8, NZ), F32),
            pltpu.VMEM((NX, 8 * NJ, NZ), F32),
            pltpu.VMEM((NP, NY, NZ), F32),
            pltpu.VMEM((NP, NY, NZ), F32),
            pltpu.VMEM((NX, 2 * NO * NY, NZ), F32),
            dma((NS, 4)),
            dma((NS, 4)),
            dma((NS, NP)),
            dma((NS, NP)),
            dma((2 * NO,)),
            dma((2 * NO,)),
            dma((2,)),
            dma((ST, 2, 4)),
            dma((ST, 2, 4)),
            dma((ST, 2, 4)),
            dma((ST, 2, 4)),
            dma((NS, 4)),
            dma((NS, 4)),
            dma((2 * NO,)),
            dma((2 * NO,)),
            dma((NP,)),
            dma((NP,)),
        ],
        compiler_params=pltpu.CompilerParams(
            collective_id=0, has_side_effects=True, vmem_limit_bytes=67043328
        ),
    )(*args)
    return costates, gradient[:, :, :LP]


def solution(mesh):
    return jax.shard_map(
        local,
        mesh=mesh,
        in_specs=(
            P(None, "obs", "gx", "gy", None),
            P(None, "gx", "gy", "obs"),
            P(None, "gx", "gy", "obs"),
            P(None, "gx", "gy", "obs"),
            P(None, "gx", "gy", "obs"),
            P(None, "obs", None),
            P("obs"),
            P("obs"),
        ),
        out_specs=(P(None, "obs", "gx", "gy", None), P("gx", "gy", "obs")),
        check_vma=False,
    )
```
